1024 devices in a mesh: gx: 128 (over y, x, z_lo), sa: 8 (over z_hi, core).
Axes of the slice: x: 8, y: 8, z: 8 (z_hi: 4, z_lo: 2; z = z_hi * 2 + z_lo), core: 2. Of those that a mesh axis runs over, the one named last changes fastest.
Arguments:
- field_in: bfloat16 [8, 128, 256, 1024], P('sa', 'gx'), may hold values from -6 to 6
- cotangent: bfloat16 [8, 128, 256, 1024], P('sa', 'gx'), may hold values from -6 to 6
- mode_weights: bfloat16 [32, 512, 64, 128], P(None, 'gx'), may hold values from -4 to 4
- point_weights: bfloat16 [64, 64], replicated, may hold values from -0.75 to 0.75
Outputs:
- field_out: bfloat16 [8, 128, 256, 1024], P('sa', 'gx')
- field_grad: bfloat16 [8, 128, 256, 1024], P('sa', 'gx')
- weight_grad: float32 [32, 512, 64, 128], P('sa', 'gx')
The draws below stay inside these ranges and needn't reach their ends.
All inputs are finite; a program needn't handle non-finite values.
Results may differ from the reference program's by a relative error of at most 0.018.
Values may be sent and summed in bfloat16 or wider, within the bound.
No kernel may reach another device: no remote copies, remote signals or barrier semaphores. Data moves between devices by JAX's collectives and lax.ppermute only.
A program may use at most 32 MiB of HBM per device.

```python
import math
import jax
import jax.numpy as jnp
from jax import lax

C = 64
KX = 32
KY = 32
KZ = 16
NY = 256
NZ = 16
NX = 128
SAMPLES = 8
MODES = 512


def steps_of(rng, shape, cuts, smallest, high):
    level, own = 1.0, jax.random.fold_in(rng, 6)
    for position, blocks in cuts:
        steps = jnp.exp(jax.random.uniform(jax.random.fold_in(own, position), (blocks,), jnp.float32, smallest / len(cuts), high / len(cuts)))
        level = level * jnp.repeat(steps, shape[position] // blocks).reshape([-1 if axis == position else 1 for axis in range(len(shape))])
    return level


def noise(own_key, shape, deviation, limit, split=(), kind=jnp.bfloat16):
    factor_of = steps_of(own_key, shape, split, -0.22, 0.18) if split else 1.0
    drawn = jax.random.normal(own_key, shape, jnp.float32) * deviation * factor_of
    return jnp.minimum(jnp.maximum(drawn, -limit), limit).astype(kind)


def setup_inputs(seed: int = 0) -> dict:
    keys = jax.random.split(jax.random.key(seed), 5)
    return {
        "field_in": noise(keys[0], (SAMPLES, NX, NY, NZ * C), 1.0, 6.0, ((0, 8), (1, 128))),
        "cotangent": noise(keys[1], (SAMPLES, NX, NY, NZ * C), 1.0, 6.0, ((0, 8), (1, 128))),
        "mode_weights": noise(keys[2], (KX, MODES, C, 2 * C), ((NX * NY * NZ // (KX * KY * KZ)) ** 0.5 * C ** -0.5), 4.0, ((1, 128),)),
        "point_weights": noise(keys[3], (C, C), C ** -0.5, 0.75),
    }


HIGHEST_PREC = lax.Precision.HIGHEST
GELU_COEF = 0.044715

def angles(freq_count, grid_count):
    frequency = jnp.arange(freq_count, dtype=jnp.int32) - freq_count // 2
    places = jnp.arange(grid_count, dtype=jnp.int32)
    turn_index = jnp.mod(frequency[:, None] * places[None, :], grid_count)
    return turn_index.astype(jnp.float32) * (2.0 * math.pi / grid_count)

def gelu_parts(pre_act):
    root_const = math.sqrt(2.0 / math.pi)
    inner_arg = root_const * (pre_act + GELU_COEF * pre_act * pre_act * pre_act)
    tangent = jnp.tanh(inner_arg)
    activated = 0.5 * pre_act * (1.0 + tangent)
    gelu_slope = 0.5 * (1.0 + tangent) + 0.5 * pre_act * (1.0 - tangent * tangent) * root_const * (1.0 + 3.0 * GELU_COEF * pre_act * pre_act)
    return (activated, gelu_slope)

def along_z_forward(data_in, table_z):
    return jnp.einsum('pyzc,kz->pykc', data_in, table_z, precision=HIGHEST_PREC)

def along_z_inverse(data_in, table_z):
    return jnp.einsum('pykc,kz->pyzc', data_in, table_z, precision=HIGHEST_PREC)

def forward_yz(local_field):
    planes = local_field.shape[0]
    theta_y = angles(KY, NY)
    table_y = jnp.concatenate([jnp.cos(theta_y), -jnp.sin(theta_y)], 0).astype(jnp.bfloat16)
    first_pass = jnp.einsum('fy,pyq->pfq', table_y.astype(jnp.float32), local_field.astype(jnp.float32), precision=HIGHEST_PREC)
    first_pass = first_pass.reshape(planes, 2, KY, NZ, C)
    theta_z = angles(KZ, NZ)
    cos_z = jnp.cos(theta_z)
    sin_z = jnp.sin(theta_z)
    real_in = first_pass[:, 0]
    imag_in = first_pass[:, 1]
    real_out = along_z_forward(real_in, cos_z) + along_z_forward(imag_in, sin_z)
    imag_out = along_z_forward(imag_in, cos_z) - along_z_forward(real_in, sin_z)
    mode_data = jnp.concatenate([real_out, imag_out], -1)
    return mode_data.reshape(planes, KY * KZ, 2 * C).astype(jnp.bfloat16)

def forward_x(mode_data, norm_scale):
    x_length, mode_block, pair_width = mode_data.shape
    channels = pair_width // 2
    theta_x = angles(KX, x_length)
    flat_data = mode_data.reshape(x_length, mode_block * pair_width)
    cos_part = jnp.dot(jnp.cos(theta_x).astype(jnp.bfloat16), flat_data, preferred_element_type=jnp.float32).reshape(KX, mode_block, pair_width)
    sin_part = jnp.dot(jnp.sin(theta_x).astype(jnp.bfloat16), flat_data, preferred_element_type=jnp.float32).reshape(KX, mode_block, pair_width)
    real_out = cos_part[..., :channels] + sin_part[..., channels:]
    imag_out = cos_part[..., channels:] - sin_part[..., :channels]
    return (jnp.concatenate([real_out, imag_out], -1) * norm_scale).astype(jnp.bfloat16)

def inverse_x(mixed_modes, x_length):
    kx_count, mode_block, pair_width = mixed_modes.shape
    channels = pair_width // 2
    theta_x = angles(kx_count, x_length).T
    flat_data = mixed_modes.reshape(kx_count, mode_block * pair_width)
    cos_part = jnp.dot(jnp.cos(theta_x).astype(jnp.bfloat16), flat_data, preferred_element_type=jnp.float32).reshape(x_length, mode_block, pair_width)
    sin_part = jnp.dot(jnp.sin(theta_x).astype(jnp.bfloat16), flat_data, preferred_element_type=jnp.float32).reshape(x_length, mode_block, pair_width)
    real_out = cos_part[..., :channels] - sin_part[..., channels:]
    imag_out = cos_part[..., channels:] + sin_part[..., :channels]
    return jnp.concatenate([real_out, imag_out], -1).astype(jnp.bfloat16)

def inverse_yz(planes_data, y_count, z_count, norm_scale):
    planes, mode_total, pair_width = planes_data.shape
    channels = pair_width // 2
    wide_data = planes_data.astype(jnp.float32).reshape(planes, KY, KZ, pair_width)
    real_in = wide_data[..., :channels]
    imag_in = wide_data[..., channels:]
    theta_z = angles(KZ, z_count)
    cos_z = jnp.cos(theta_z)
    sin_z = jnp.sin(theta_z)
    real_mid = along_z_inverse(real_in, cos_z) - along_z_inverse(imag_in, sin_z)
    imag_mid = along_z_inverse(imag_in, cos_z) + along_z_inverse(real_in, sin_z)
    stacked = jnp.concatenate([real_mid, imag_mid], 1).reshape(planes, 2 * KY, z_count * channels)
    theta_y = angles(KY, y_count)
    table_y = jnp.concatenate([jnp.cos(theta_y), -jnp.sin(theta_y)], 0)
    return jnp.einsum('pfq,fy->pyq', stacked, table_y, precision=HIGHEST_PREC) * norm_scale

def mix_forward(coeffs, weights_wide):
    channels = weights_wide.shape[2]
    wide_coeffs = coeffs.astype(jnp.float32)
    real_part = jnp.einsum('kmc,kmcp->kmp', wide_coeffs[..., :channels], weights_wide, precision=HIGHEST_PREC)
    imag_part = jnp.einsum('kmc,kmcp->kmp', wide_coeffs[..., channels:], weights_wide, precision=HIGHEST_PREC)
    out_real = real_part[..., :channels] - imag_part[..., channels:]
    out_imag = real_part[..., channels:] + imag_part[..., :channels]
    return jnp.concatenate([out_real, out_imag], -1).astype(jnp.bfloat16)

def mix_backward(coeffs, weights_wide):
    channels = weights_wide.shape[2]
    wide_coeffs = coeffs.astype(jnp.float32)
    swapped = jnp.concatenate([wide_coeffs[..., channels:], -wide_coeffs[..., :channels]], -1)
    first_half = jnp.einsum('kmp,kmcp->kmc', wide_coeffs, weights_wide, precision=HIGHEST_PREC)
    second_half = jnp.einsum('kmp,kmcp->kmc', swapped, weights_wide, precision=HIGHEST_PREC)
    return jnp.concatenate([first_half, second_half], -1).astype(jnp.bfloat16)

def pointwise(local_field, weights_small):
    channels = weights_small.shape[0]
    cells = local_field.reshape(-1, channels)
    return jnp.dot(cells, weights_small, preferred_element_type=jnp.float32).reshape(local_field.shape)

def sample_sum(left_side, right_side):
    channels = left_side.shape[-1] // 2
    left_wide = left_side.astype(jnp.float32)
    right_wide = right_side.astype(jnp.float32)
    left_real = left_wide[..., :channels]
    left_imag = left_wide[..., channels:]
    right_real = right_wide[..., :channels]
    right_imag = right_wide[..., channels:]

    def outer_sum(left_op, right_op):
        return jnp.einsum('skmc,skmo->kmco', left_op, right_op, precision=HIGHEST_PREC)
    real_sum = outer_sum(left_real, right_real) + outer_sum(left_imag, right_imag)
    imag_sum = outer_sum(left_real, right_imag) - outer_sum(left_imag, right_real)
    return jnp.concatenate([real_sum, imag_sum], -1)

def reference(field_in, cotangent, mode_weights, point_weights):
    weights_wide = mode_weights.astype(jnp.float32)
    norm_scale = 1.0 / math.sqrt(NX * NY * NZ)

    def one_sample(pair_in):
        local_field, local_cot = pair_in
        coeffs_in = forward_x(forward_yz(local_field), norm_scale)
        spec_out = inverse_yz(inverse_x(mix_forward(coeffs_in, weights_wide), NX), NY, NZ, norm_scale)
        pre_act = spec_out + pointwise(local_field, point_weights)
        activated, gelu_slope = gelu_parts(pre_act)
        out_grad = (local_cot.astype(jnp.float32) * gelu_slope).astype(jnp.bfloat16)
        coeffs_grad = forward_x(forward_yz(out_grad), norm_scale)
        spec_grad = inverse_yz(inverse_x(mix_backward(coeffs_grad, weights_wide), NX), NY, NZ, norm_scale)
        field_grad = (spec_grad + pointwise(out_grad, point_weights.T)).astype(jnp.bfloat16)
        return (activated.astype(jnp.bfloat16), field_grad, coeffs_in, coeffs_grad)
    field_out, field_grad, coeffs_all, grads_all = lax.map(one_sample, (field_in, cotangent))

    def grad_row(row_pair):
        left_row, right_row = row_pair
        return sample_sum(left_row[:, None], right_row[:, None])[0]
    weight_grad = lax.map(grad_row, (coeffs_all.transpose(1, 0, 2, 3), grads_all.transpose(1, 0, 2, 3)))
    return (field_out, field_grad, weight_grad)
```

```python
import math

import jax
import jax.numpy as jnp
from jax import lax
from jax.sharding import PartitionSpec as P

KY = 32
KZ = 16


HIGHEST_PREC = lax.Precision.HIGHEST
GELU_COEF = 0.044715


def angles(freq_count, grid_count):
    frequency = jnp.arange(freq_count, dtype=jnp.int32) - freq_count // 2
    places = jnp.arange(grid_count, dtype=jnp.int32)
    turn_index = jnp.mod(frequency[:, None] * places[None, :], grid_count)
    return turn_index.astype(jnp.float32) * (2.0 * math.pi / grid_count)


def gelu_parts(pre_act):
    root_const = math.sqrt(2.0 / math.pi)
    inner_arg = root_const * (pre_act + GELU_COEF * pre_act * pre_act * pre_act)
    tangent = jnp.tanh(inner_arg)
    activated = 0.5 * pre_act * (1.0 + tangent)
    gelu_slope = 0.5 * (1.0 + tangent) + 0.5 * pre_act * (1.0 - tangent * tangent) * root_const * (
        1.0 + 3.0 * GELU_COEF * pre_act * pre_act
    )
    return (activated, gelu_slope)


def along_z_forward(data_in, table_z):
    return jnp.einsum("pyzc,kz->pykc", data_in, table_z, precision=HIGHEST_PREC)


def along_z_inverse(data_in, table_z):
    return jnp.einsum("pykc,kz->pyzc", data_in, table_z, precision=HIGHEST_PREC)


def forward_yz(local_field, channels):
    planes, y_count, last_width = local_field.shape
    z_count = last_width // channels
    theta_y = angles(KY, y_count)
    table_y = jnp.concatenate([jnp.cos(theta_y), -jnp.sin(theta_y)], 0).astype(jnp.bfloat16)
    first_pass = jnp.einsum("fy,pyq->pfq", table_y, local_field, preferred_element_type=jnp.float32)
    first_pass = first_pass.reshape(planes, 2, KY, z_count, channels)
    theta_z = angles(KZ, z_count)
    cos_z = jnp.cos(theta_z)
    sin_z = jnp.sin(theta_z)
    real_in = first_pass[:, 0]
    imag_in = first_pass[:, 1]
    real_out = along_z_forward(real_in, cos_z) + along_z_forward(imag_in, sin_z)
    imag_out = along_z_forward(imag_in, cos_z) - along_z_forward(real_in, sin_z)
    mode_data = jnp.concatenate([real_out, imag_out], -1)
    return mode_data.reshape(planes, KY * KZ, 2 * channels).astype(jnp.bfloat16)


def forward_x(mode_data, kx_count, norm_scale):
    x_length, mode_block, pair_width = mode_data.shape
    channels = pair_width // 2
    theta_x = angles(kx_count, x_length)
    flat_data = mode_data.reshape(x_length, mode_block * pair_width)
    cos_part = jnp.dot(
        jnp.cos(theta_x).astype(jnp.bfloat16), flat_data, preferred_element_type=jnp.float32
    ).reshape(kx_count, mode_block, pair_width)
    sin_part = jnp.dot(
        jnp.sin(theta_x).astype(jnp.bfloat16), flat_data, preferred_element_type=jnp.float32
    ).reshape(kx_count, mode_block, pair_width)
    real_out = cos_part[..., :channels] + sin_part[..., channels:]
    imag_out = cos_part[..., channels:] - sin_part[..., :channels]
    return (jnp.concatenate([real_out, imag_out], -1) * norm_scale).astype(jnp.bfloat16)


def inverse_x(mixed_modes, x_length):
    kx_count, mode_block, pair_width = mixed_modes.shape
    channels = pair_width // 2
    theta_x = angles(kx_count, x_length).T
    flat_data = mixed_modes.reshape(kx_count, mode_block * pair_width)
    cos_part = jnp.dot(
        jnp.cos(theta_x).astype(jnp.bfloat16), flat_data, preferred_element_type=jnp.float32
    ).reshape(x_length, mode_block, pair_width)
    sin_part = jnp.dot(
        jnp.sin(theta_x).astype(jnp.bfloat16), flat_data, preferred_element_type=jnp.float32
    ).reshape(x_length, mode_block, pair_width)
    real_out = cos_part[..., :channels] - sin_part[..., channels:]
    imag_out = cos_part[..., channels:] + sin_part[..., :channels]
    return jnp.concatenate([real_out, imag_out], -1).astype(jnp.bfloat16)


def inverse_yz(planes_data, y_count, z_count, norm_scale):
    planes, mode_total, pair_width = planes_data.shape
    channels = pair_width // 2
    wide_data = planes_data.astype(jnp.float32).reshape(planes, KY, KZ, pair_width)
    real_in = wide_data[..., :channels]
    imag_in = wide_data[..., channels:]
    theta_z = angles(KZ, z_count)
    cos_z = jnp.cos(theta_z)
    sin_z = jnp.sin(theta_z)
    real_mid = along_z_inverse(real_in, cos_z) - along_z_inverse(imag_in, sin_z)
    imag_mid = along_z_inverse(imag_in, cos_z) + along_z_inverse(real_in, sin_z)
    stacked = jnp.concatenate([real_mid, imag_mid], 1).reshape(planes, 2 * KY, z_count * channels)
    theta_y = angles(KY, y_count)
    table_y = jnp.concatenate([jnp.cos(theta_y), -jnp.sin(theta_y)], 0)
    return jnp.einsum("pfq,fy->pyq", stacked, table_y, precision=HIGHEST_PREC) * norm_scale


def mix_forward(coeffs, weights_local):
    channels = weights_local.shape[2]
    real_part = jnp.einsum(
        "kmc,kmcp->kmp", coeffs[..., :channels], weights_local, preferred_element_type=jnp.float32
    )
    imag_part = jnp.einsum(
        "kmc,kmcp->kmp", coeffs[..., channels:], weights_local, preferred_element_type=jnp.float32
    )
    out_real = real_part[..., :channels] - imag_part[..., channels:]
    out_imag = real_part[..., channels:] + imag_part[..., :channels]
    return jnp.concatenate([out_real, out_imag], -1).astype(jnp.bfloat16)


def mix_backward(coeffs, weights_local):
    channels = weights_local.shape[2]
    swapped = jnp.concatenate([coeffs[..., channels:], -coeffs[..., :channels]], -1)
    first_half = jnp.einsum(
        "kmp,kmcp->kmc", coeffs, weights_local, preferred_element_type=jnp.float32
    )
    second_half = jnp.einsum(
        "kmp,kmcp->kmc", swapped, weights_local, preferred_element_type=jnp.float32
    )
    return jnp.concatenate([first_half, second_half], -1).astype(jnp.bfloat16)


def pointwise(local_field, weights_small):
    planes, y_count, last_width = local_field.shape
    channels = weights_small.shape[0]
    paired = jnp.kron(jnp.eye(2, dtype=weights_small.dtype), weights_small)
    cell_pairs = local_field.reshape(planes * y_count * last_width // (2 * channels), 2 * channels)
    return jnp.dot(cell_pairs, paired, preferred_element_type=jnp.float32).reshape(
        planes, y_count, last_width
    )


def sample_sum(left_side, right_side):
    channels = left_side.shape[-1] // 2
    left_real = left_side[..., :channels]
    left_imag = left_side[..., channels:]
    right_real = right_side[..., :channels]
    right_imag = right_side[..., channels:]

    def outer_sum(left_op, right_op):
        return jnp.einsum("skmc,skmo->kmco", left_op, right_op, preferred_element_type=jnp.float32)

    real_sum = outer_sum(left_real, right_real) + outer_sum(left_imag, right_imag)
    imag_sum = outer_sum(left_real, right_imag) - outer_sum(left_imag, right_real)
    return jnp.concatenate([real_sum, imag_sum], -1)


def exchange(slot_buffer):
    return lax.all_to_all(slot_buffer, "gx", split_axis=0, concat_axis=0, tiled=True)


def toward_modes(mode_data):
    planes, mode_total, pair_width = mode_data.shape
    group_size = lax.axis_size("gx")
    slot_buffer = mode_data.reshape(
        planes, group_size, mode_total // group_size, pair_width
    ).transpose(1, 0, 2, 3)
    return exchange(slot_buffer).reshape(
        planes * group_size, mode_total // group_size, pair_width
    )


def toward_planes(back_planes):
    x_length, mode_block, pair_width = back_planes.shape
    group_size = lax.axis_size("gx")
    slot_buffer = back_planes.reshape(group_size, x_length // group_size, mode_block, pair_width)
    arrived = exchange(slot_buffer)
    return arrived.transpose(1, 0, 2, 3).reshape(
        x_length // group_size, group_size * mode_block, pair_width
    )


def on_device(field_in, cotangent, mode_weights, point_weights):
    local_field = field_in[0]
    planes, y_count, last_width = local_field.shape
    channels = point_weights.shape[0]
    z_count = last_width // channels
    kx_count = mode_weights.shape[0]
    x_length = planes * lax.axis_size("gx")
    norm_scale = 1.0 / math.sqrt(x_length * y_count * z_count)
    coeffs_in = forward_x(toward_modes(forward_yz(local_field, channels)), kx_count, norm_scale)
    mixed_modes = mix_forward(coeffs_in, mode_weights)
    spec_out = inverse_yz(
        toward_planes(inverse_x(mixed_modes, x_length)), y_count, z_count, norm_scale
    )
    pre_act = spec_out + pointwise(local_field, point_weights)
    activated, gelu_slope = gelu_parts(pre_act)
    out_grad = (cotangent[0].astype(jnp.float32) * gelu_slope).astype(jnp.bfloat16)
    coeffs_grad = forward_x(toward_modes(forward_yz(out_grad, channels)), kx_count, norm_scale)
    back_modes = mix_backward(coeffs_grad, mode_weights)
    spec_grad = inverse_yz(
        toward_planes(inverse_x(back_modes, x_length)), y_count, z_count, norm_scale
    )
    field_grad = (spec_grad + pointwise(out_grad, point_weights.T)).astype(jnp.bfloat16)
    shared_in, shared_grad = (
        lax.all_to_all(coeffs_in[None], "sa", split_axis=1, concat_axis=0, tiled=True),
        lax.all_to_all(coeffs_grad[None], "sa", split_axis=1, concat_axis=0, tiled=True),
    )
    weight_grad = sample_sum(shared_in, shared_grad)
    return (activated.astype(jnp.bfloat16)[None], field_grad[None], weight_grad)


def solution(mesh):
    in_specs = (
        P("sa", "gx", None, None),
        P("sa", "gx", None, None),
        P(None, "gx", None, None),
        P(),
    )
    out_specs = (P("sa", "gx", None, None), P("sa", "gx", None, None), P("sa", "gx", None, None))
    return jax.shard_map(
        on_device, mesh=mesh, in_specs=in_specs, out_specs=out_specs, check_vma=False
    )
```

```python
import math

import jax
import jax.numpy as jnp
import numpy as np
from jax import lax
from jax.experimental import pallas as pl
from jax.experimental.pallas import tpu as pltpu
from jax.sharding import PartitionSpec as P

KY = 32
KZ = 16
GELU_COEF = 0.044715
VMEM_BYTES = 40 << 20


def angles(freq_count, grid_count):
    frequency = np.arange(freq_count) - freq_count // 2
    turn_index = np.mod(frequency[:, None] * np.arange(grid_count)[None, :], grid_count)
    return turn_index.astype(np.float32) * np.float32(2.0 * math.pi / grid_count)


def tables_y(y_count):
    theta = angles(KY, y_count)
    return np.concatenate([np.cos(theta), -np.sin(theta)], 0).astype(np.float32)


def forward_table_y(y_count):
    return tables_y(y_count).astype(jnp.bfloat16)


def inverse_table_y(y_count):
    table = tables_y(y_count).T
    high = table.astype(jnp.bfloat16)
    low = (table - high.astype(np.float32)).astype(jnp.bfloat16)
    return np.concatenate([high, high, low], 1)


def tables_x(kx_count, x_length, mode_block):
    theta = angles(kx_count, x_length)
    same = np.eye(mode_block, dtype=np.float32)
    cos_wide = np.kron(np.cos(theta), same)
    sin_wide = np.kron(np.sin(theta), same)
    forward = np.concatenate([cos_wide, sin_wide], 0).astype(jnp.bfloat16)
    inverse = np.concatenate([cos_wide.T, sin_wide.T], 1).astype(jnp.bfloat16)
    return forward, inverse


def dot(left, right):
    return jnp.dot(left, right, preferred_element_type=jnp.float32)


def lanes_of(shape):
    return lax.broadcasted_iota(jnp.int32, shape, 1)


def halves_swapped(pair):
    return pltpu.roll(pair, pair.shape[1] // 2, 1)


def quarter_turn(pair, sign):
    low = lanes_of(pair.shape) < pair.shape[1] // 2
    swapped = halves_swapped(pair)
    return jnp.where(low, -swapped, swapped) if sign > 0 else jnp.where(low, swapped, -swapped)


def fourier(parts, sign):
    count = len(parts)
    if count == 1:
        return parts
    even = fourier(parts[0::2], sign)
    odd = fourier(parts[1::2], sign)
    lower, upper = [], []
    for k in range(count // 2):
        turned = odd[k]
        if 4 * k == count:
            turned = quarter_turn(turned, sign)
        elif k:
            angle = 2.0 * math.pi * k / count
            turned = math.cos(angle) * turned + math.sin(angle) * quarter_turn(turned, sign)
        lower.append(even[k] + turned)
        upper.append(even[k] - turned)
    return lower + upper


def modes_from(first_pass, wide_modes, modes_out):
    width = modes_out.shape[1]
    low = lanes_of((8, width)) < width // 2
    for block in range(KY // 8):
        parts = []
        for column in range(KZ // 2):
            lanes = pl.ds(column * width, width)
            real = first_pass[pl.ds(block * 8, 8), lanes]
            imag = first_pass[pl.ds(KY + block * 8, 8), lanes]
            parts.append(jnp.where(low, real, halves_swapped(imag)))
            parts.append(jnp.where(low, halves_swapped(real), imag))
        spectrum = fourier(parts, -1)
        for kz in range(KZ):
            wide_modes[pl.ds(block * 8 * KZ + kz, 8, stride=KZ), :] = spectrum[(kz + KZ // 2) % KZ]
    modes_out[...] = wide_modes[...].astype(modes_out.dtype)


def stacked_from(planes, wide_modes, stacked, norm_scale):
    width = planes.shape[1]
    low = lanes_of((8, width)) < width // 2
    wide_modes[...] = planes[...].astype(jnp.float32)
    for block in range(KY // 8):
        parts = [
            wide_modes[pl.ds(block * 8 * KZ + (k + KZ // 2) % KZ, 8, stride=KZ), :] for k in range(KZ)
        ]
        grid = fourier(parts, 1)
        for column in range(KZ // 2):
            lanes = pl.ds(column * width, width)
            first = grid[2 * column] * norm_scale
            second = grid[2 * column + 1] * norm_scale
            stacked[pl.ds(block * 8, 8), lanes] = jnp.where(low, first, halves_swapped(second))
            stacked[pl.ds(KY + block * 8, 8), lanes] = jnp.where(low, halves_swapped(first), second)


def three_terms(stacked, lanes):
    value = stacked[:, lanes]
    high = value.astype(jnp.bfloat16)
    low = (value - high.astype(jnp.float32)).astype(jnp.bfloat16)
    return jnp.concatenate([high, low, high], 0)


def forward_yz_kernel(table_y, field, modes_out, first_pass, wide_modes):
    first_pass[...] = dot(table_y[...], field[...])
    modes_from(first_pass, wide_modes, modes_out)


def middle_kernel(
    norm_scale, planes, inverse_y, table_y, paired, field, cotangent,
    modes_out, field_out, out_grad, stacked, first_pass, wide_modes,
):
    stacked_from(planes, wide_modes, stacked, norm_scale)
    root_const = math.sqrt(2.0 / math.pi)
    width = paired.shape[0]
    rows_per = 64
    for column in range(field.shape[1] // width):
        lanes = pl.ds(column * width, width)
        terms = three_terms(stacked, lanes)
        for start in range(0, field.shape[0], rows_per):
            rows = pl.ds(start, rows_per)
            pre_act = dot(inverse_y[rows, :], terms) + dot(field[rows, lanes], paired[...])
            square = pre_act * pre_act
            tangent = jnp.tanh(pre_act * (root_const + root_const * GELU_COEF * square))
            half = 0.5 + 0.5 * tangent
            activated = pre_act * half
            slope = half + activated * (1.0 - tangent) * (root_const + 3.0 * root_const * GELU_COEF * square)
            field_out[rows, lanes] = activated.astype(field_out.dtype)
            out_grad[rows, lanes] = (cotangent[rows, lanes].astype(jnp.float32) * slope).astype(out_grad.dtype)
        first_pass[:, lanes] = dot(table_y[...], out_grad[:, lanes])
    modes_from(first_pass, wide_modes, modes_out)


def last_kernel(norm_scale, planes, inverse_y, paired, out_grad, field_grad, stacked, wide_modes):
    stacked_from(planes, wide_modes, stacked, norm_scale)
    width = paired.shape[0]
    rows_per = 128
    for column in range(out_grad.shape[1] // width):
        lanes = pl.ds(column * width, width)
        terms = three_terms(stacked, lanes)
        for start in range(0, out_grad.shape[0], rows_per):
            rows = pl.ds(start, rows_per)
            grad = dot(inverse_y[rows, :], terms) + dot(out_grad[rows, lanes], paired[...])
            field_grad[rows, lanes] = grad.astype(field_grad.dtype)


def coeffs_of(forward_x, mode_data, norm_scale):
    both = dot(forward_x[...], mode_data[...])
    count = both.shape[0] // 2
    return ((both[:count] + quarter_turn(both[count:], -1)) * norm_scale).astype(jnp.bfloat16)


def planes_of(inverse_x, mixed):
    turned = quarter_turn(mixed.astype(jnp.float32), 1).astype(jnp.bfloat16)
    return dot(inverse_x[...], jnp.concatenate([mixed, turned], 0)).astype(jnp.bfloat16)


def own_block(shape, channels):
    row = lax.broadcasted_iota(jnp.int32, shape, 0)
    return lanes_of(shape) // channels == row % 8


def mixed_forward(coeffs, weights, mixed):
    count, width = coeffs.shape
    channels = width // 2
    mine = own_block((8, 8 * channels), channels)
    low = lanes_of((8, width)) < channels
    for start in range(0, count, 8):
        pair = coeffs[start : start + 8].astype(jnp.float32)
        swapped = halves_swapped(pair)
        real = jnp.where(low, pair, swapped)
        imag = jnp.where(low, swapped, pair)
        spread = jnp.concatenate(
            [jnp.where(mine, jnp.concatenate([part] * 4, 1), 0.0) for part in (real, imag)], 0
        ).astype(jnp.bfloat16)
        both = dot(spread, weights[pl.ds(start * channels, 8 * channels), :])
        mixed[pl.ds(start, 8), :] = both[:8] + quarter_turn(both[8:], 1)


def mixed_backward(coeffs, weights, mixed):
    count, width = coeffs.shape
    channels = width // 2
    mine = own_block((8, 8 * channels), channels)
    low = lanes_of((8, width)) < channels
    for start in range(0, count, 8):
        pair = coeffs[start : start + 8].astype(jnp.float32)
        sides = jnp.concatenate([pair, quarter_turn(pair, -1)], 0).astype(jnp.bfloat16)
        every = lax.dot_general(
            sides,
            weights[pl.ds(start * channels, 8 * channels), :],
            (((1,), (1,)), ((), ())),
            preferred_element_type=jnp.float32,
        )
        folded = []
        for half in (every[:8], every[8:]):
            own = jnp.where(mine, half, 0.0)
            total = sum(own[:, at * width : (at + 1) * width] for at in range(4))
            folded.append(total + halves_swapped(total))
        mixed[pl.ds(start, 8), :] = jnp.where(low, folded[0], folded[1])


def mix_forward_kernel(norm_scale, mode_data, forward_x, inverse_x, weights, coeffs_out, planes_out, mixed):
    coeffs = coeffs_of(forward_x, mode_data, norm_scale)
    coeffs_out[...] = coeffs
    mixed_forward(coeffs, weights, mixed)
    planes_out[...] = planes_of(inverse_x, mixed[...].astype(jnp.bfloat16))


def forward_x_kernel(norm_scale, mode_data, forward_x, coeffs_out):
    coeffs_out[...] = coeffs_of(forward_x, mode_data, norm_scale)


def mix_backward_kernel(coeffs_in, inverse_x, weights, planes_out, mixed):
    mixed_backward(coeffs_in[...], weights, mixed)
    planes_out[...] = planes_of(inverse_x, mixed[...].astype(jnp.bfloat16))


def call(kernel, operands, outs, scratch, name):
    single = isinstance(outs, tuple)
    flat = [outs] if single else list(outs)
    whole = pl.BlockSpec(memory_space=pltpu.VMEM)
    result = pl.pallas_call(
        kernel,
        name=name,
        out_shape=[jax.ShapeDtypeStruct(shape, jnp.bfloat16) for shape in flat],
        in_specs=[whole] * len(operands),
        out_specs=[whole] * len(flat),
        scratch_shapes=[pltpu.VMEM(shape, jnp.float32) for shape in scratch],
        compiler_params=pltpu.CompilerParams(vmem_limit_bytes=VMEM_BYTES),
    )(*operands)
    return result[0] if single else result


def exchange(rows):
    count = lax.axis_size("gx")
    slots = rows.reshape(count, rows.shape[0] // count, rows.shape[1])
    return lax.all_to_all(slots, "gx", split_axis=0, concat_axis=0, tiled=True).reshape(rows.shape)


def sample_sum(left_side, right_side):
    samples, kx_count, mode_block, width = left_side.shape
    channels = width // 2
    left = left_side.reshape(samples, kx_count, mode_block, 2, channels)
    swapped = jnp.concatenate([right_side[..., channels:], -right_side[..., :channels]], -1)
    right = jnp.stack([right_side, swapped], 3)
    return jnp.einsum("skmtc,skmtp->kmcp", left, right, preferred_element_type=jnp.float32)


def on_device(field_in, cotangent, mode_weights, point_weights):
    field = field_in.reshape(field_in.shape[-2:])
    cotangent_rows = cotangent.reshape(field.shape)
    y_count, last_width = field.shape
    channels = point_weights.shape[0]
    kx_count, mode_block = mode_weights.shape[:2]
    x_length = lax.axis_size("gx")
    samples = lax.axis_size("sa")
    z_count = last_width // channels
    norm_scale = 1.0 / math.sqrt(x_length * y_count * z_count)
    width = 2 * channels
    mode_total = KY * KZ
    table_y = forward_table_y(y_count)
    inverse_y = inverse_table_y(y_count)
    forward_x, inverse_x = tables_x(kx_count, x_length, mode_block)
    table_y, inverse_y, forward_x, inverse_x = map(jnp.asarray, (table_y, inverse_y, forward_x, inverse_x))
    weights = mode_weights.reshape(-1, width)
    four = jnp.eye(4, dtype=point_weights.dtype)
    paired = jnp.kron(four, point_weights)
    paired_back = jnp.kron(four, point_weights.T)
    scaled = lambda kernel: lambda *refs: kernel(norm_scale, *refs)
    rows = kx_count * mode_block
    planar = (mode_total, width)
    stacked = (2 * KY, last_width)

    modes = call(forward_yz_kernel, (table_y, field), planar, [stacked, planar], "forward_yz")
    coeffs_in, planes = call(
        scaled(mix_forward_kernel),
        (exchange(modes), forward_x, inverse_x, weights),
        [(rows, width), planar],
        [(rows, width)],
        "mix_forward",
    )
    modes, field_out, out_grad = call(
        scaled(middle_kernel),
        (exchange(planes), inverse_y, table_y, paired, field, cotangent_rows),
        [planar, field.shape, field.shape],
        [stacked, stacked, planar],
        "middle",
    )
    coeffs_grad = call(
        scaled(forward_x_kernel), (exchange(modes), forward_x), (rows, width), [], "forward_x"
    )
    both = jnp.stack([coeffs_in, coeffs_grad], 0).reshape(2, samples, kx_count // samples, mode_block, width)
    shared = lax.all_to_all(both, "sa", split_axis=1, concat_axis=1, tiled=True)
    planes = call(
        mix_backward_kernel, (coeffs_grad, inverse_x, weights), planar, [(rows, width)], "mix_backward"
    )
    field_grad = call(
        scaled(last_kernel),
        (exchange(planes), inverse_y, paired_back, out_grad),
        field.shape,
        [stacked, planar],
        "last",
    )
    weight_grad = sample_sum(shared[0], shared[1])
    return (
        field_out.reshape(field_in.shape),
        field_grad.reshape(field_in.shape),
        weight_grad,
    )


def solution(mesh):
    in_specs = (
        P("sa", "gx", None, None),
        P("sa", "gx", None, None),
        P(None, "gx", None, None),
        P(),
    )
    out_specs = (P("sa", "gx", None, None), P("sa", "gx", None, None), P("sa", "gx", None, None))
    return jax.shard_map(
        on_device, mesh=mesh, in_specs=in_specs, out_specs=out_specs, check_vma=False
    )
```

```python
import math

import jax
import jax.numpy as jnp
import numpy as np
from jax import lax
from jax.experimental import pallas as pl
from jax.experimental.pallas import tpu as pltpu
from jax.sharding import PartitionSpec as P

KY = 32
KZ = 16
GELU_COEF = 0.044715
VMEM_BYTES = 40 << 20


def angles(freq_count, grid_count):
    frequency = np.arange(freq_count) - freq_count // 2
    turn_index = np.mod(frequency[:, None] * np.arange(grid_count)[None, :], grid_count)
    return turn_index.astype(np.float32) * np.float32(2.0 * math.pi / grid_count)


def tables_y(y_count):
    theta = angles(KY, y_count)
    return np.concatenate([np.cos(theta), -np.sin(theta)], 0).astype(np.float32)


def forward_table_y(y_count):
    return tables_y(y_count).astype(jnp.bfloat16)


def inverse_table_y(y_count):
    table = tables_y(y_count).T
    high = table.astype(jnp.bfloat16)
    low = (table - high.astype(np.float32)).astype(jnp.bfloat16)
    return np.concatenate([high, high, low], 1)


def table_x(kx_count, x_length, mode_block):
    theta = angles(kx_count, x_length)
    same = np.eye(mode_block, dtype=np.float32)
    cos_wide = np.kron(np.cos(theta), same)
    sin_wide = np.kron(np.sin(theta), same)
    return np.concatenate([cos_wide, sin_wide], 0).astype(jnp.bfloat16)


def dot(left, right):
    return jnp.dot(left, right, preferred_element_type=jnp.float32)


def lanes_of(shape):
    return lax.broadcasted_iota(jnp.int32, shape, 1)


def halves_swapped(pair):
    return pltpu.roll(pair, pair.shape[1] // 2, 1)


def quarter_turn(pair, sign):
    low = lanes_of(pair.shape) < pair.shape[1] // 2
    swapped = halves_swapped(pair)
    return jnp.where(low, -swapped, swapped) if sign > 0 else jnp.where(low, swapped, -swapped)


def fourier(parts, sign):
    count = len(parts)
    if count == 1:
        return parts
    even = fourier(parts[0::2], sign)
    odd = fourier(parts[1::2], sign)
    lower, upper = [], []
    for k in range(count // 2):
        turned = odd[k]
        if 4 * k == count:
            turned = quarter_turn(turned, sign)
        elif k:
            angle = 2.0 * math.pi * k / count
            turned = math.cos(angle) * turned + math.sin(angle) * quarter_turn(turned, sign)
        lower.append(even[k] + turned)
        upper.append(even[k] - turned)
    return lower + upper


def modes_from(first_pass, wide_modes, modes_out):
    width = modes_out.shape[1]
    low = lanes_of((8, width)) < width // 2
    for block in range(KY // 8):
        parts = []
        for column in range(KZ // 2):
            lanes = pl.ds(column * width, width)
            real = first_pass[pl.ds(block * 8, 8), lanes]
            imag = first_pass[pl.ds(KY + block * 8, 8), lanes]
            parts.append(jnp.where(low, real, halves_swapped(imag)))
            parts.append(jnp.where(low, halves_swapped(real), imag))
        spectrum = fourier(parts, -1)
        for kz in range(KZ):
            wide_modes[pl.ds(block * 8 * KZ + kz, 8, stride=KZ), :] = spectrum[(kz + KZ // 2) % KZ]
    modes_out[...] = wide_modes[...].astype(modes_out.dtype)


def stacked_from(planes, wide_modes, stacked, norm_scale):
    width = planes.shape[1]
    low = lanes_of((8, width)) < width // 2
    wide_modes[...] = planes[...].astype(jnp.float32)
    for block in range(KY // 8):
        parts = [
            wide_modes[pl.ds(block * 8 * KZ + (k + KZ // 2) % KZ, 8, stride=KZ), :] for k in range(KZ)
        ]
        grid = fourier(parts, 1)
        for column in range(KZ // 2):
            lanes = pl.ds(column * width, width)
            first = grid[2 * column] * norm_scale
            second = grid[2 * column + 1] * norm_scale
            stacked[pl.ds(block * 8, 8), lanes] = jnp.where(low, first, halves_swapped(second))
            stacked[pl.ds(KY + block * 8, 8), lanes] = jnp.where(low, halves_swapped(first), second)


def three_terms(stacked, lanes):
    value = stacked[:, lanes]
    high = value.astype(jnp.bfloat16)
    low = (value - high.astype(jnp.float32)).astype(jnp.bfloat16)
    return jnp.concatenate([high, low, high], 0)


def forward_yz_kernel(table_y, field, modes_out, first_pass, wide_modes):
    first_pass[...] = dot(table_y[...], field[...])
    modes_from(first_pass, wide_modes, modes_out)


def middle_kernel(
    norm_scale, planes, inverse_y, table_y, paired, field, cotangent,
    modes_out, field_out, out_grad, stacked, first_pass, wide_modes,
):
    stacked_from(planes, wide_modes, stacked, norm_scale)
    root_const = math.sqrt(2.0 / math.pi)
    width = paired.shape[0]
    rows_per = 64
    for column in range(field.shape[1] // width):
        lanes = pl.ds(column * width, width)
        terms = three_terms(stacked, lanes)
        for start in range(0, field.shape[0], rows_per):
            rows = pl.ds(start, rows_per)
            pre_act = dot(inverse_y[rows, :], terms) + dot(field[rows, lanes], paired[...])
            square = pre_act * pre_act
            tangent = jnp.tanh(pre_act * (root_const + root_const * GELU_COEF * square))
            half = 0.5 + 0.5 * tangent
            activated = pre_act * half
            slope = half + activated * (1.0 - tangent) * (root_const + 3.0 * root_const * GELU_COEF * square)
            field_out[rows, lanes] = activated.astype(field_out.dtype)
            out_grad[rows, lanes] = (cotangent[rows, lanes].astype(jnp.float32) * slope).astype(out_grad.dtype)
        first_pass[:, lanes] = dot(table_y[...], out_grad[:, lanes])
    modes_from(first_pass, wide_modes, modes_out)


def last_kernel(norm_scale, planes, inverse_y, paired, out_grad, field_grad, stacked, wide_modes):
    stacked_from(planes, wide_modes, stacked, norm_scale)
    width = paired.shape[0]
    rows_per = 128
    for column in range(out_grad.shape[1] // width):
        lanes = pl.ds(column * width, width)
        terms = three_terms(stacked, lanes)
        for start in range(0, out_grad.shape[0], rows_per):
            rows = pl.ds(start, rows_per)
            grad = dot(inverse_y[rows, :], terms) + dot(out_grad[rows, lanes], paired[...])
            field_grad[rows, lanes] = grad.astype(field_grad.dtype)


def coeffs_of(along_x, mode_data, norm_scale):
    both = dot(along_x[...], mode_data[...])
    count = both.shape[0] // 2
    return ((both[:count] + quarter_turn(both[count:], -1)) * norm_scale).astype(jnp.bfloat16)


def planes_of(along_x, mixed):
    turned = quarter_turn(mixed.astype(jnp.float32), 1).astype(jnp.bfloat16)
    return lax.dot_general(
        along_x[...],
        jnp.concatenate([mixed, turned], 0),
        (((0,), (0,)), ((), ())),
        preferred_element_type=jnp.float32,
    ).astype(jnp.bfloat16)


def own_block(shape, channels):
    row = lax.broadcasted_iota(jnp.int32, shape, 0)
    return lanes_of(shape) // channels == row % 8


def mixed_forward(coeffs, weights, mixed):
    count, width = coeffs.shape
    channels = width // 2
    mine = own_block((8, 8 * channels), channels)
    low = lanes_of((8, width)) < channels
    for start in range(0, count, 8):
        pair = coeffs[start : start + 8].astype(jnp.float32)
        swapped = halves_swapped(pair)
        real = jnp.where(low, pair, swapped)
        imag = jnp.where(low, swapped, pair)
        spread = jnp.concatenate(
            [jnp.where(mine, jnp.concatenate([part] * 4, 1), 0.0) for part in (real, imag)], 0
        ).astype(jnp.bfloat16)
        both = dot(spread, weights[pl.ds(start * channels, 8 * channels), :])
        mixed[pl.ds(start, 8), :] = both[:8] + quarter_turn(both[8:], 1)


def mixed_backward(coeffs, weights, mixed):
    count, width = coeffs.shape
    channels = width // 2
    mine = own_block((8, 8 * channels), channels)
    low = lanes_of((8, width)) < channels
    for start in range(0, count, 8):
        pair = coeffs[start : start + 8].astype(jnp.float32)
        sides = jnp.concatenate([pair, quarter_turn(pair, -1)], 0).astype(jnp.bfloat16)
        every = lax.dot_general(
            sides,
            weights[pl.ds(start * channels, 8 * channels), :],
            (((1,), (1,)), ((), ())),
            preferred_element_type=jnp.float32,
        )
        folded = []
        for half in (every[:8], every[8:]):
            own = jnp.where(mine, half, 0.0)
            total = sum(own[:, at * width : (at + 1) * width] for at in range(4))
            folded.append(total + halves_swapped(total))
        mixed[pl.ds(start, 8), :] = jnp.where(low, folded[0], folded[1])


def mix_forward_kernel(norm_scale, mode_data, along_x, weights, coeffs_out, planes_out, mixed):
    coeffs = coeffs_of(along_x, mode_data, norm_scale)
    coeffs_out[...] = coeffs
    mixed_forward(coeffs, weights, mixed)
    planes_out[...] = planes_of(along_x, mixed[...].astype(jnp.bfloat16))


def forward_x_kernel(norm_scale, mode_data, along_x, coeffs_out):
    coeffs_out[...] = coeffs_of(along_x, mode_data, norm_scale)


def mix_backward_kernel(coeffs_in, along_x, weights, planes_out, mixed):
    mixed_backward(coeffs_in[...], weights, mixed)
    planes_out[...] = planes_of(along_x, mixed[...].astype(jnp.bfloat16))


def call(kernel, operands, outs, scratch, name):
    single = isinstance(outs, tuple)
    flat = [outs] if single else list(outs)
    whole = pl.BlockSpec(memory_space=pltpu.VMEM)
    result = pl.pallas_call(
        kernel,
        name=name,
        out_shape=[jax.ShapeDtypeStruct(shape, jnp.bfloat16) for shape in flat],
        in_specs=[whole] * len(operands),
        out_specs=[whole] * len(flat),
        scratch_shapes=[pltpu.VMEM(shape, jnp.float32) for shape in scratch],
        compiler_params=pltpu.CompilerParams(vmem_limit_bytes=VMEM_BYTES),
    )(*operands)
    return result[0] if single else result


def exchange(rows):
    count = lax.axis_size("gx")
    slots = rows.reshape(count, rows.shape[0] // count, rows.shape[1])
    return lax.all_to_all(slots, "gx", split_axis=0, concat_axis=0, tiled=True).reshape(rows.shape)


def swap_samples(both):
    count = lax.axis_size("sa")
    mine = lax.axis_index("sa")
    core = jnp.bitwise_and(mine, 1)
    place = jnp.right_shift(mine, 1)
    blocks = both.reshape((2, count // 2, 2, both.shape[1] // count) + both.shape[2:])
    kept = lax.dynamic_index_in_dim(blocks, core, 2, keepdims=False)
    given = lax.dynamic_index_in_dim(blocks, 1 - core, 2, keepdims=False)
    taken = lax.ppermute(given, "sa", [(i, i ^ 1) for i in range(count)])
    pair = jnp.stack([kept, taken], 0)
    arrived = [lax.dynamic_index_in_dim(pair, place, 2, keepdims=False)]
    for step in range(1, count // 2):
        block = lax.dynamic_index_in_dim(pair, jnp.bitwise_xor(place, step), 2, keepdims=False)
        arrived.append(lax.ppermute(block, "sa", [(i, i ^ 2 * step) for i in range(count)]))
    return jnp.concatenate(arrived, 0)


def sample_sum(left_side, right_side):
    samples, kx_count, mode_block, width = left_side.shape
    channels = width // 2
    left = left_side.reshape(samples, kx_count, mode_block, 2, channels)
    swapped = jnp.concatenate([right_side[..., channels:], -right_side[..., :channels]], -1)
    right = jnp.stack([right_side, swapped], 3)
    return jnp.einsum("skmtc,skmtp->kmcp", left, right, preferred_element_type=jnp.float32)


def on_device(field_in, cotangent, mode_weights, point_weights):
    field = field_in.reshape(field_in.shape[-2:])
    cotangent_rows = cotangent.reshape(field.shape)
    y_count, last_width = field.shape
    channels = point_weights.shape[0]
    kx_count, mode_block = mode_weights.shape[:2]
    x_length = lax.axis_size("gx")
    samples = lax.axis_size("sa")
    z_count = last_width // channels
    norm_scale = 1.0 / math.sqrt(x_length * y_count * z_count)
    width = 2 * channels
    mode_total = KY * KZ
    table_y = forward_table_y(y_count)
    inverse_y = inverse_table_y(y_count)
    along_x = table_x(kx_count, x_length, mode_block)
    table_y, inverse_y, along_x = map(jnp.asarray, (table_y, inverse_y, along_x))
    weights = mode_weights.reshape(-1, width)
    four = jnp.eye(4, dtype=point_weights.dtype)
    paired = jnp.kron(four, point_weights)
    paired_back = jnp.kron(four, point_weights.T)
    scaled = lambda kernel: lambda *refs: kernel(norm_scale, *refs)
    rows = kx_count * mode_block
    planar = (mode_total, width)
    stacked = (2 * KY, last_width)

    modes = call(forward_yz_kernel, (table_y, field), planar, [stacked, planar], "forward_yz")
    coeffs_in, planes = call(
        scaled(mix_forward_kernel),
        (exchange(modes), along_x, weights),
        [(rows, width), planar],
        [(rows, width)],
        "mix_forward",
    )
    modes, field_out, out_grad = call(
        scaled(middle_kernel),
        (exchange(planes), inverse_y, table_y, paired, field, cotangent_rows),
        [planar, field.shape, field.shape],
        [stacked, stacked, planar],
        "middle",
    )
    coeffs_grad = call(
        scaled(forward_x_kernel), (exchange(modes), along_x), (rows, width), [], "forward_x"
    )
    planes = call(
        mix_backward_kernel, (coeffs_grad, along_x, weights), planar, [(rows, width)], "mix_backward"
    )
    both = jnp.stack([coeffs_in, coeffs_grad], 0).reshape(2, kx_count, mode_block, width)
    shared = swap_samples(both)
    field_grad = call(
        scaled(last_kernel),
        (exchange(planes), inverse_y, paired_back, out_grad),
        field.shape,
        [stacked, planar],
        "last",
    )
    shared, field_grad = lax.optimization_barrier((shared, field_grad))
    weight_grad = sample_sum(shared[:, 0], shared[:, 1])
    return (
        field_out.reshape(field_in.shape),
        field_grad.reshape(field_in.shape),
        weight_grad,
    )


def solution(mesh):
    in_specs = (
        P("sa", "gx", None, None),
        P("sa", "gx", None, None),
        P(None, "gx", None, None),
        P(),
    )
    out_specs = (P("sa", "gx", None, None), P("sa", "gx", None, None), P("sa", "gx", None, None))
    return jax.shard_map(
        on_device, mesh=mesh, in_specs=in_specs, out_specs=out_specs, check_vma=False
    )
```

```python
import math

import jax
import jax.numpy as jnp
import numpy as np
from jax import lax
from jax.experimental import pallas as pl
from jax.experimental.pallas import tpu as pltpu
from jax.sharding import PartitionSpec as P

KY = 32
KZ = 16
GELU_COEF = 0.044715
LARGE_BYTES = 56 << 20
SMALL_BYTES = 16 << 20
PIECES = 4


def angles(freq_count, grid_count):
    frequency = np.arange(freq_count) - freq_count // 2
    turn_index = np.mod(frequency[:, None] * np.arange(grid_count)[None, :], grid_count)
    return turn_index.astype(np.float32) * np.float32(2.0 * math.pi / grid_count)


def tables_y(y_count):
    theta = angles(KY, y_count)
    return np.concatenate([np.cos(theta), -np.sin(theta)], 0).astype(np.float32)


def forward_table_y(y_count):
    return tables_y(y_count).astype(jnp.bfloat16)


def inverse_table_y(y_count):
    table = tables_y(y_count).T
    high = table.astype(jnp.bfloat16)
    low = (table - high.astype(np.float32)).astype(jnp.bfloat16)
    return np.concatenate([high, high, low], 1)


def table_x(kx_count, x_length, mode_block):
    theta = angles(kx_count, x_length)
    same = np.eye(mode_block, dtype=np.float32)
    cos_wide = np.kron(np.cos(theta), same)
    sin_wide = np.kron(np.sin(theta), same)
    return np.concatenate([cos_wide, sin_wide], 0).astype(jnp.bfloat16)


def dot(left, right):
    return jnp.dot(left, right, preferred_element_type=jnp.float32)


def lanes_of(shape):
    return lax.broadcasted_iota(jnp.int32, shape, 1)


def halves_swapped(pair):
    return pltpu.roll(pair, pair.shape[1] // 2, 1)


def quarter_turn(pair, sign):
    low = lanes_of(pair.shape) < pair.shape[1] // 2
    swapped = halves_swapped(pair)
    return jnp.where(low, -swapped, swapped) if sign > 0 else jnp.where(low, swapped, -swapped)


def fourier(parts, sign):
    count = len(parts)
    if count == 1:
        return parts
    even = fourier(parts[0::2], sign)
    odd = fourier(parts[1::2], sign)
    lower, upper = [], []
    for k in range(count // 2):
        turned = odd[k]
        if 4 * k == count:
            turned = quarter_turn(turned, sign)
        elif k:
            angle = 2.0 * math.pi * k / count
            turned = math.cos(angle) * turned + math.sin(angle) * quarter_turn(turned, sign)
        lower.append(even[k] + turned)
        upper.append(even[k] - turned)
    return lower + upper


class Fetched:
    def __init__(self, source, target, semaphores, first, pieces=1, axis=0):
        size = source.shape[axis] // pieces
        self.copies = []
        for at in range(pieces):
            part = pl.ds(at * size, size)
            index = (part,) if axis == 0 else (slice(None), part)
            self.copies.append(
                pltpu.make_async_copy(source.at[index], target.at[index], semaphores.at[first + at])
            )

    def start(self, at=None):
        for copy in self.copies if at is None else self.copies[at : at + 1]:
            copy.start()

    def wait(self, at=None):
        for copy in self.copies if at is None else self.copies[at : at + 1]:
            copy.wait()


def modes_from(first_pass, wide_modes, modes_out, store):
    width = modes_out.shape[1]
    low = lanes_of((8, width)) < width // 2
    for block in range(KY // 8):
        parts = []
        for column in range(KZ // 2):
            lanes = pl.ds(column * width, width)
            real = first_pass[pl.ds(block * 8, 8), lanes]
            imag = first_pass[pl.ds(KY + block * 8, 8), lanes]
            parts.append(jnp.where(low, real, halves_swapped(imag)))
            parts.append(jnp.where(low, halves_swapped(real), imag))
        spectrum = fourier(parts, -1)
        for kz in range(KZ):
            wide_modes[pl.ds(block * 8 * KZ + kz, 8, stride=KZ), :] = spectrum[(kz + KZ // 2) % KZ]
        rows = pl.ds(block * 8 * KZ, 8 * KZ)
        modes_out[rows, :] = wide_modes[rows, :].astype(modes_out.dtype)
        store.start(block)


def stacked_from(planes, wide_modes, stacked, norm_scale):
    width = planes.shape[1]
    low = lanes_of((8, width)) < width // 2
    wide_modes[...] = planes[...].astype(jnp.float32)
    for block in range(KY // 8):
        parts = [
            wide_modes[pl.ds(block * 8 * KZ + (k + KZ // 2) % KZ, 8, stride=KZ), :] for k in range(KZ)
        ]
        grid = fourier(parts, 1)
        for column in range(KZ // 2):
            lanes = pl.ds(column * width, width)
            first = grid[2 * column] * norm_scale
            second = grid[2 * column + 1] * norm_scale
            stacked[pl.ds(block * 8, 8), lanes] = jnp.where(low, first, halves_swapped(second))
            stacked[pl.ds(KY + block * 8, 8), lanes] = jnp.where(low, halves_swapped(first), second)


def three_terms(stacked, lanes):
    value = stacked[:, lanes]
    high = value.astype(jnp.bfloat16)
    low = (value - high.astype(jnp.float32)).astype(jnp.bfloat16)
    return jnp.concatenate([high, low, high], 0)


def paired_of(point_weights):
    channels = point_weights.shape[0]
    wide = jnp.concatenate([point_weights[...].astype(jnp.float32)] * 4, 1)
    tall = jnp.concatenate([wide] * 4, 0)
    row = lax.broadcasted_iota(jnp.int32, tall.shape, 0)
    return jnp.where(row // channels == lanes_of(tall.shape) // channels, tall, 0.0).astype(jnp.bfloat16)


def forward_yz_kernel(
    table_in, field_in, modes_hbm, table_y, field, modes_out, first_pass, wide_modes, semaphores
):
    table_fetch = Fetched(table_in, table_y, semaphores, 0)
    field_fetch = Fetched(field_in, field, semaphores, 1, PIECES, 1)
    store = Fetched(modes_out, modes_hbm, semaphores, 1 + PIECES, PIECES)
    table_fetch.start()
    field_fetch.start()
    table_fetch.wait()
    width = field.shape[1] // PIECES
    for column in range(PIECES):
        lanes = pl.ds(column * width, width)
        field_fetch.wait(column)
        first_pass[:, lanes] = dot(table_y[...], field[:, lanes])
    modes_from(first_pass, wide_modes, modes_out, store)
    store.wait()


def middle_kernel(
    norm_scale,
    planes_in, inverse_in, table_in, point_in, field_in, cotangent_in,
    modes_hbm, field_out_hbm, out_grad_hbm,
    planes, inverse_y, table_y, point_weights, field, cotangent, modes_out, field_out, out_grad,
    stacked, first_pass, wide_modes, semaphores,
):
    small = [
        Fetched(source, target, semaphores, at)
        for at, (source, target) in enumerate(
            ((planes_in, planes), (inverse_in, inverse_y), (point_in, point_weights), (table_in, table_y))
        )
    ]
    field_fetch = Fetched(field_in, field, semaphores, 4, PIECES, 1)
    cotangent_fetch = Fetched(cotangent_in, cotangent, semaphores, 4 + PIECES, PIECES, 1)
    modes_store = Fetched(modes_out, modes_hbm, semaphores, 4 + 2 * PIECES, PIECES)
    out_store = Fetched(field_out, field_out_hbm, semaphores, 4 + 3 * PIECES, PIECES, 1)
    grad_store = Fetched(out_grad, out_grad_hbm, semaphores, 4 + 4 * PIECES, PIECES, 1)
    for fetch in small:
        fetch.start()
    for at in range(PIECES):
        field_fetch.start(at)
        cotangent_fetch.start(at)
    small[2].wait()
    paired = paired_of(point_weights)
    small[0].wait()
    stacked_from(planes, wide_modes, stacked, norm_scale)
    small[1].wait()
    small[3].wait()
    root_const = math.sqrt(2.0 / math.pi)
    width = field.shape[1] // PIECES
    rows_per = 64
    for column in range(PIECES):
        lanes = pl.ds(column * width, width)
        terms = three_terms(stacked, lanes)
        field_fetch.wait(column)
        cotangent_fetch.wait(column)
        for start in range(0, field.shape[0], rows_per):
            rows = pl.ds(start, rows_per)
            pre_act = dot(inverse_y[rows, :], terms) + dot(field[rows, lanes], paired)
            square = pre_act * pre_act
            tangent = jnp.tanh(pre_act * (root_const + root_const * GELU_COEF * square))
            half = 0.5 + 0.5 * tangent
            activated = pre_act * half
            slope = half + activated * (1.0 - tangent) * (root_const + 3.0 * root_const * GELU_COEF * square)
            field_out[rows, lanes] = activated.astype(field_out.dtype)
            out_grad[rows, lanes] = (cotangent[rows, lanes].astype(jnp.float32) * slope).astype(out_grad.dtype)
        grad_store.start(column)
        out_store.start(column)
        first_pass[:, lanes] = dot(table_y[...], out_grad[:, lanes])
    modes_from(first_pass, wide_modes, modes_out, modes_store)
    grad_store.wait()
    out_store.wait()
    modes_store.wait()


def last_kernel(norm_scale, planes, inverse_y, point_weights, out_grad, field_grad, stacked, wide_modes):
    paired = paired_of(point_weights)
    stacked_from(planes, wide_modes, stacked, norm_scale)
    width = paired.shape[0]
    rows_per = 128
    for column in range(out_grad.shape[1] // width):
        lanes = pl.ds(column * width, width)
        terms = three_terms(stacked, lanes)
        for start in range(0, out_grad.shape[0], rows_per):
            rows = pl.ds(start, rows_per)
            mixed = lax.dot_general(
                out_grad[rows, lanes], paired, (((1,), (1,)), ((), ())), preferred_element_type=jnp.float32
            )
            field_grad[rows, lanes] = (dot(inverse_y[rows, :], terms) + mixed).astype(field_grad.dtype)


def coeffs_of(along_x, mode_data, norm_scale):
    both = dot(along_x[...], mode_data[...])
    count = both.shape[0] // 2
    return ((both[:count] + quarter_turn(both[count:], -1)) * norm_scale).astype(jnp.bfloat16)


def store_planes(along_x, mixed, planes_out, store):
    mixed = mixed[...]
    turned = quarter_turn(mixed.astype(jnp.bfloat16).astype(jnp.float32), 1).astype(jnp.bfloat16)
    terms = jnp.concatenate([mixed.astype(jnp.bfloat16), turned], 0)
    size = planes_out.shape[0] // PIECES
    for piece in range(PIECES):
        rows = pl.ds(piece * size, size)
        planes_out[rows, :] = lax.dot_general(
            along_x[:, rows], terms, (((0,), (0,)), ((), ())), preferred_element_type=jnp.float32
        ).astype(jnp.bfloat16)
        store.start(piece)
    store.wait()


def own_block(shape, channels):
    row = lax.broadcasted_iota(jnp.int32, shape, 0)
    return lanes_of(shape) // channels == row % 8


def mixed_forward(coeffs, weights, weights_fetch, mixed):
    count, width = coeffs.shape
    channels = width // 2
    mine = own_block((8, 8 * channels), channels)
    low = lanes_of((8, width)) < channels
    for start in range(0, count, 8):
        if start % (count // PIECES) == 0:
            weights_fetch.wait(start // (count // PIECES))
        pair = coeffs[start : start + 8].astype(jnp.float32)
        swapped = halves_swapped(pair)
        real = jnp.where(low, pair, swapped)
        imag = jnp.where(low, swapped, pair)
        spread = jnp.concatenate(
            [jnp.where(mine, jnp.concatenate([part] * 4, 1), 0.0) for part in (real, imag)], 0
        ).astype(jnp.bfloat16)
        both = dot(spread, weights[pl.ds(start * channels, 8 * channels), :])
        mixed[pl.ds(start, 8), :] = both[:8] + quarter_turn(both[8:], 1)


def mixed_backward(coeffs, weights, weights_fetch, mixed):
    count, width = coeffs.shape
    channels = width // 2
    mine = own_block((8, 8 * channels), channels)
    low = lanes_of((8, width)) < channels
    for start in range(0, count, 8):
        if start % (count // PIECES) == 0:
            weights_fetch.wait(start // (count // PIECES))
        pair = coeffs[start : start + 8].astype(jnp.float32)
        sides = jnp.concatenate([pair, quarter_turn(pair, -1)], 0).astype(jnp.bfloat16)
        every = lax.dot_general(
            sides,
            weights[pl.ds(start * channels, 8 * channels), :],
            (((1,), (1,)), ((), ())),
            preferred_element_type=jnp.float32,
        )
        folded = []
        for half in (every[:8], every[8:]):
            own = jnp.where(mine, half, 0.0)
            total = sum(own[:, at * width : (at + 1) * width] for at in range(4))
            folded.append(total + halves_swapped(total))
        mixed[pl.ds(start, 8), :] = jnp.where(low, folded[0], folded[1])


def mix_forward_kernel(
    norm_scale,
    mode_in, along_in, weights_in,
    coeffs_hbm, planes_hbm,
    mode_data, along_x, weights, coeffs_out, planes_out, mixed, semaphores,
):
    mode_fetch = Fetched(mode_in, mode_data, semaphores, 0)
    along_fetch = Fetched(along_in, along_x, semaphores, 1)
    coeffs_store = Fetched(coeffs_out, coeffs_hbm, semaphores, 2)
    weights_fetch = Fetched(weights_in, weights, semaphores, 3, PIECES)
    store = Fetched(planes_out, planes_hbm, semaphores, 3 + PIECES, PIECES)
    mode_fetch.start()
    along_fetch.start()
    weights_fetch.start()
    mode_fetch.wait()
    along_fetch.wait()
    coeffs = coeffs_of(along_x, mode_data, norm_scale)
    coeffs_out[...] = coeffs
    coeffs_store.start()
    mixed_forward(coeffs, weights, weights_fetch, mixed)
    store_planes(along_x, mixed, planes_out, store)
    coeffs_store.wait()


def mix_backward_kernel(
    norm_scale, samples,
    core, mode_in, along_in, weights_in, coeffs_in_hbm,
    kept, given, planes_hbm,
    mode_data, along_x, weights, coeffs_in, planes_out, mixed, semaphores,
):
    mode_fetch = Fetched(mode_in, mode_data, semaphores, 0)
    along_fetch = Fetched(along_in, along_x, semaphores, 1)
    coeffs_fetch = Fetched(coeffs_in_hbm, coeffs_in, semaphores, 2)
    weights_fetch = Fetched(weights_in, weights, semaphores, 3, PIECES)
    store = Fetched(planes_out, planes_hbm, semaphores, 3 + PIECES, PIECES)
    mode_fetch.start()
    along_fetch.start()
    coeffs_fetch.start()
    weights_fetch.start()
    mode_fetch.wait()
    along_fetch.wait()
    coeffs = coeffs_of(along_x, mode_data, norm_scale)
    coeffs_fetch.wait()
    first_core = core[0] == 0
    size = coeffs.shape[0] // samples
    for side, values in enumerate((coeffs_in[...], coeffs)):
        for place in range(samples // 2):
            even = values[2 * place * size : (2 * place + 1) * size].astype(jnp.float32)
            odd = values[(2 * place + 1) * size : (2 * place + 2) * size].astype(jnp.float32)
            rows = pl.ds((side * (samples // 2) + place) * size, size)
            kept[rows, :] = jnp.where(first_core, even, odd).astype(jnp.bfloat16)
            given[rows, :] = jnp.where(first_core, odd, even).astype(jnp.bfloat16)
    mixed_backward(coeffs, weights, weights_fetch, mixed)
    store_planes(along_x, mixed, planes_out, store)


def call(kernel, operands, outs, scratch, name):
    copied = [pltpu.VMEM(array.shape, array.dtype) for array in operands] + [
        pltpu.VMEM(shape, jnp.bfloat16) for shape in outs
    ]
    return pl.pallas_call(
        kernel,
        name=name,
        out_shape=[jax.ShapeDtypeStruct(shape, jnp.bfloat16) for shape in outs],
        in_specs=[pl.BlockSpec(memory_space=pl.ANY)] * len(operands),
        out_specs=[pl.BlockSpec(memory_space=pl.ANY)] * len(outs),
        scratch_shapes=copied
        + [pltpu.VMEM(shape, jnp.float32) for shape in scratch]
        + [pltpu.SemaphoreType.DMA((4 + 5 * PIECES,))],
        compiler_params=pltpu.CompilerParams(vmem_limit_bytes=LARGE_BYTES),
    )(*operands)


def call_mix_backward(norm_scale, samples, core, operands, rows):
    whole = pl.BlockSpec(memory_space=pltpu.VMEM)
    width = operands[0].shape[1]
    count = operands[3].shape[0]
    outs = [(count, width), (count, width), operands[0].shape]
    return pl.pallas_call(
        lambda *refs: mix_backward_kernel(norm_scale, samples, *refs),
        name="mix_backward",
        out_shape=[jax.ShapeDtypeStruct(shape, jnp.bfloat16) for shape in outs],
        in_specs=[pl.BlockSpec(memory_space=pltpu.SMEM)] + [pl.BlockSpec(memory_space=pl.ANY)] * len(operands),
        out_specs=[whole, whole, pl.BlockSpec(memory_space=pl.ANY)],
        scratch_shapes=[pltpu.VMEM(array.shape, array.dtype) for array in operands]
        + [pltpu.VMEM(outs[2], jnp.bfloat16), pltpu.VMEM(rows, jnp.float32)]
        + [pltpu.SemaphoreType.DMA((4 + 5 * PIECES,))],
        compiler_params=pltpu.CompilerParams(vmem_limit_bytes=LARGE_BYTES),
    )(core, *operands)


def call_last(norm_scale, operands, shape, scratch):
    whole = pl.BlockSpec(memory_space=pltpu.VMEM)
    return pl.pallas_call(
        lambda *refs: last_kernel(norm_scale, *refs),
        name="last",
        out_shape=jax.ShapeDtypeStruct(shape, jnp.bfloat16),
        in_specs=[whole] * len(operands),
        out_specs=whole,
        scratch_shapes=[pltpu.VMEM(shape, jnp.float32) for shape in scratch],
        compiler_params=pltpu.CompilerParams(vmem_limit_bytes=SMALL_BYTES),
    )(*operands)


def exchange(rows):
    count = lax.axis_size("gx")
    slots = rows.reshape(count, rows.shape[0] // count, rows.shape[1])
    return lax.all_to_all(slots, "gx", split_axis=0, concat_axis=0, tiled=True).reshape(rows.shape)


def swap_samples(kept, given, mine):
    count = lax.axis_size("sa")
    width = kept.shape[1]
    taken = lax.ppermute(given, "sa", [(i, i ^ 1) for i in range(count)])
    pair = jnp.stack([kept, taken], 0).reshape(2, 2, count // 2, -1, width)
    place = jnp.right_shift(mine, 1)
    arrived = [lax.dynamic_index_in_dim(pair, place, 2, keepdims=False)]
    for step in range(1, count // 2):
        block = lax.dynamic_index_in_dim(pair, jnp.bitwise_xor(place, step), 2, keepdims=False)
        arrived.append(lax.ppermute(block, "sa", [(i, i ^ 2 * step) for i in range(count)]))
    return jnp.concatenate(arrived, 0)


def sample_sum(left_side, right_side):
    samples, kx_count, mode_block, width = left_side.shape
    channels = width // 2
    left = left_side.reshape(samples, kx_count, mode_block, 2, channels)
    swapped = jnp.concatenate([right_side[..., channels:], -right_side[..., :channels]], -1)
    right = jnp.stack([right_side, swapped], 3)
    return jnp.einsum("skmtc,skmtp->kmcp", left, right, preferred_element_type=jnp.float32)


def on_device(field_in, cotangent, mode_weights, point_weights):
    field = field_in.reshape(field_in.shape[-2:])
    cotangent_rows = cotangent.reshape(field.shape)
    y_count, last_width = field.shape
    channels = point_weights.shape[0]
    kx_count, mode_block = mode_weights.shape[:2]
    x_length = lax.axis_size("gx")
    samples = lax.axis_size("sa")
    z_count = last_width // channels
    norm_scale = 1.0 / math.sqrt(x_length * y_count * z_count)
    width = 2 * channels
    mode_total = KY * KZ
    table_y = forward_table_y(y_count)
    inverse_y = inverse_table_y(y_count)
    along_x = table_x(kx_count, x_length, mode_block)
    table_y, inverse_y, along_x = map(jnp.asarray, (table_y, inverse_y, along_x))
    weights = mode_weights.reshape(-1, width)
    scaled = lambda kernel: lambda *refs: kernel(norm_scale, *refs)
    rows = kx_count * mode_block
    planar = (mode_total, width)
    stacked = (2 * KY, last_width)
    mine = lax.axis_index("sa")
    core, field = lax.optimization_barrier((jnp.bitwise_and(mine, 1).reshape(1), field))

    (modes,) = call(forward_yz_kernel, (table_y, field), [planar], [stacked, planar], "forward_yz")
    coeffs_in, planes = call(
        scaled(mix_forward_kernel),
        (exchange(modes), along_x, weights),
        [(rows, width), planar],
        [(rows, width)],
        "mix_forward",
    )
    modes, field_out, out_grad = call(
        scaled(middle_kernel),
        (exchange(planes), inverse_y, table_y, point_weights, field, cotangent_rows),
        [planar, field.shape, field.shape],
        [stacked, stacked, planar],
        "middle",
    )
    kept, given, planes = call_mix_backward(
        norm_scale,
        samples,
        core,
        (exchange(modes), along_x, weights, coeffs_in),
        (rows, width),
    )
    shared = swap_samples(kept, given, mine).reshape(
        samples, 2, kx_count // samples, mode_block, width
    )
    field_grad = call_last(
        norm_scale, (exchange(planes), inverse_y, point_weights, out_grad), field.shape, [stacked, planar]
    )
    shared, field_grad = lax.optimization_barrier((shared, field_grad))
    weight_grad = sample_sum(shared[:, 0], shared[:, 1])
    return (
        field_out.reshape(field_in.shape),
        field_grad.reshape(field_in.shape),
        weight_grad,
    )


def solution(mesh):
    in_specs = (
        P("sa", "gx", None, None),
        P("sa", "gx", None, None),
        P(None, "gx", None, None),
        P(),
    )
    out_specs = (P("sa", "gx", None, None), P("sa", "gx", None, None), P("sa", "gx", None, None))
    return jax.shard_map(
        on_device, mesh=mesh, in_specs=in_specs, out_specs=out_specs, check_vma=False
    )
```

```python
import math

import jax
import jax.numpy as jnp
import numpy as np
from jax import lax
from jax.experimental import pallas as pl
from jax.experimental.pallas import tpu as pltpu
from jax.sharding import PartitionSpec as P

KY = 32
KZ = 16
GELU_COEF = 0.044715
FIRST_BYTES = 16 << 20
SMALL_BYTES = 16 << 20
PIECES = 4


def angles(freq_count, grid_count):
    frequency = np.arange(freq_count) - freq_count // 2
    turn_index = np.mod(frequency[:, None] * np.arange(grid_count)[None, :], grid_count)
    return turn_index.astype(np.float32) * np.float32(2.0 * math.pi / grid_count)


def tables_y(y_count):
    theta = angles(KY, y_count)
    return np.concatenate([np.cos(theta), -np.sin(theta)], 0).astype(np.float32)


def forward_table_y(y_count):
    return tables_y(y_count).astype(jnp.bfloat16)


def inverse_table_y(y_count):
    table = tables_y(y_count).T
    high = table.astype(jnp.bfloat16)
    low = (table - high.astype(np.float32)).astype(jnp.bfloat16)
    return np.concatenate([high, high, low], 1)


def table_x(kx_count, x_length, mode_block):
    theta = angles(kx_count, x_length)
    same = np.eye(mode_block, dtype=np.float32)
    cos_wide = np.kron(np.cos(theta), same)
    sin_wide = np.kron(np.sin(theta), same)
    return np.concatenate([cos_wide, sin_wide], 0).astype(jnp.bfloat16)


def dot(left, right):
    return jnp.dot(left, right, preferred_element_type=jnp.float32)


def lanes_of(shape):
    return lax.broadcasted_iota(jnp.int32, shape, 1)


def halves_swapped(pair):
    return pltpu.roll(pair, pair.shape[1] // 2, 1)


def quarter_turn(pair, sign):
    low = lanes_of(pair.shape) < pair.shape[1] // 2
    swapped = halves_swapped(pair)
    return jnp.where(low, -swapped, swapped) if sign > 0 else jnp.where(low, swapped, -swapped)


def fourier(parts, sign):
    count = len(parts)
    if count == 1:
        return parts
    even = fourier(parts[0::2], sign)
    odd = fourier(parts[1::2], sign)
    lower, upper = [], []
    for k in range(count // 2):
        turned = odd[k]
        if 4 * k == count:
            turned = quarter_turn(turned, sign)
        elif k:
            angle = 2.0 * math.pi * k / count
            turned = math.cos(angle) * turned + math.sin(angle) * quarter_turn(turned, sign)
        lower.append(even[k] + turned)
        upper.append(even[k] - turned)
    return lower + upper


class Fetched:
    def __init__(self, source, target, semaphores, first, pieces=1, axis=0):
        size = source.shape[axis] // pieces
        self.copies = []
        for at in range(pieces):
            part = pl.ds(at * size, size)
            index = (part,) if axis == 0 else (slice(None), part)
            self.copies.append(
                pltpu.make_async_copy(source.at[index], target.at[index], semaphores.at[first + at])
            )

    def start(self, at=None):
        for copy in self.copies if at is None else self.copies[at : at + 1]:
            copy.start()

    def wait(self, at=None):
        for copy in self.copies if at is None else self.copies[at : at + 1]:
            copy.wait()


def modes_from(first_pass, wide_modes, modes_out):
    width = modes_out.shape[1]
    low = lanes_of((8, width)) < width // 2
    for block in range(KY // 8):
        parts = []
        for column in range(KZ // 2):
            lanes = pl.ds(column * width, width)
            real = first_pass[pl.ds(block * 8, 8), lanes]
            imag = first_pass[pl.ds(KY + block * 8, 8), lanes]
            parts.append(jnp.where(low, real, halves_swapped(imag)))
            parts.append(jnp.where(low, halves_swapped(real), imag))
        spectrum = fourier(parts, -1)
        for kz in range(KZ):
            wide_modes[pl.ds(block * 8 * KZ + kz, 8, stride=KZ), :] = spectrum[(kz + KZ // 2) % KZ]
        rows = pl.ds(block * 8 * KZ, 8 * KZ)
        modes_out[rows, :] = wide_modes[rows, :].astype(modes_out.dtype)


def stacked_from(planes, wide_modes, stacked, norm_scale):
    width = planes.shape[1]
    low = lanes_of((8, width)) < width // 2
    wide_modes[...] = planes[...].astype(jnp.float32)
    for block in range(KY // 8):
        parts = [
            wide_modes[pl.ds(block * 8 * KZ + (k + KZ // 2) % KZ, 8, stride=KZ), :] for k in range(KZ)
        ]
        grid = fourier(parts, 1)
        for column in range(KZ // 2):
            lanes = pl.ds(column * width, width)
            first = grid[2 * column] * norm_scale
            second = grid[2 * column + 1] * norm_scale
            stacked[pl.ds(block * 8, 8), lanes] = jnp.where(low, first, halves_swapped(second))
            stacked[pl.ds(KY + block * 8, 8), lanes] = jnp.where(low, halves_swapped(first), second)


def three_terms(stacked, lanes):
    value = stacked[:, lanes]
    high = value.astype(jnp.bfloat16)
    low = (value - high.astype(jnp.float32)).astype(jnp.bfloat16)
    return jnp.concatenate([high, low, high], 0)


def paired_of(point_weights):
    channels = point_weights.shape[0]
    wide = jnp.concatenate([point_weights[...].astype(jnp.float32)] * 4, 1)
    tall = jnp.concatenate([wide] * 4, 0)
    row = lax.broadcasted_iota(jnp.int32, tall.shape, 0)
    return jnp.where(row // channels == lanes_of(tall.shape) // channels, tall, 0.0).astype(jnp.bfloat16)


def forward_yz_kernel(*refs):
    count = (len(refs) - 4) // 2
    sources, (modes_out, *targets) = refs[:count], refs[count : 2 * count + 1]
    first_pass, wide_modes, semaphores = refs[2 * count + 1 :]
    fetches = [
        Fetched(source, target, semaphores, at, PIECES if at == 0 else 1, 1)
        if at == 0
        else Fetched(source, target, semaphores, PIECES + at)
        for at, (source, target) in enumerate(zip(sources, targets))
    ]
    fetches[1].start()
    fetches[0].start()
    for fetch in fetches[2:]:
        fetch.start()
    field, table_y = targets[:2]
    fetches[1].wait()
    width = field.shape[1] // PIECES
    for column in range(PIECES):
        lanes = pl.ds(column * width, width)
        fetches[0].wait(column)
        first_pass[:, lanes] = dot(table_y[...], field[:, lanes])
    modes_from(first_pass, wide_modes, modes_out)
    for fetch in fetches[2:]:
        fetch.wait()


def middle_kernel(
    norm_scale, planes, inverse_y, table_y, point_weights, field, cotangent,
    modes_out, field_out, out_grad, stacked, first_pass, wide_modes,
):
    paired = paired_of(point_weights)
    stacked_from(planes, wide_modes, stacked, norm_scale)
    root_const = math.sqrt(2.0 / math.pi)
    width = field.shape[1] // PIECES
    rows_per = 64
    for column in range(PIECES):
        lanes = pl.ds(column * width, width)
        terms = three_terms(stacked, lanes)
        for start in range(0, field.shape[0], rows_per):
            rows = pl.ds(start, rows_per)
            pre_act = dot(inverse_y[rows, :], terms) + dot(field[rows, lanes], paired)
            square = pre_act * pre_act
            tangent = jnp.tanh(pre_act * (root_const + root_const * GELU_COEF * square))
            half = 0.5 + 0.5 * tangent
            activated = pre_act * half
            slope = half + activated * (1.0 - tangent) * (root_const + 3.0 * root_const * GELU_COEF * square)
            field_out[rows, lanes] = activated.astype(field_out.dtype)
            out_grad[rows, lanes] = (cotangent[rows, lanes].astype(jnp.float32) * slope).astype(out_grad.dtype)
        first_pass[:, lanes] = dot(table_y[...], out_grad[:, lanes])
    modes_from(first_pass, wide_modes, modes_out)


def last_kernel(norm_scale, planes, inverse_y, point_weights, out_grad, field_grad, stacked, wide_modes):
    paired = paired_of(point_weights)
    stacked_from(planes, wide_modes, stacked, norm_scale)
    width = paired.shape[0]
    rows_per = 128
    for column in range(out_grad.shape[1] // width):
        lanes = pl.ds(column * width, width)
        terms = three_terms(stacked, lanes)
        for start in range(0, out_grad.shape[0], rows_per):
            rows = pl.ds(start, rows_per)
            mixed = lax.dot_general(
                out_grad[rows, lanes], paired, (((1,), (1,)), ((), ())), preferred_element_type=jnp.float32
            )
            field_grad[rows, lanes] = (dot(inverse_y[rows, :], terms) + mixed).astype(field_grad.dtype)


def coeffs_of(along_x, mode_data, norm_scale):
    both = dot(along_x[...], mode_data[...])
    count = both.shape[0] // 2
    return ((both[:count] + quarter_turn(both[count:], -1)) * norm_scale).astype(jnp.bfloat16)


def store_planes(along_x, mixed, planes_out):
    mixed = mixed[...]
    turned = quarter_turn(mixed.astype(jnp.bfloat16).astype(jnp.float32), 1).astype(jnp.bfloat16)
    terms = jnp.concatenate([mixed.astype(jnp.bfloat16), turned], 0)
    size = planes_out.shape[0] // PIECES
    for piece in range(PIECES):
        rows = pl.ds(piece * size, size)
        planes_out[rows, :] = lax.dot_general(
            along_x[:, rows], terms, (((0,), (0,)), ((), ())), preferred_element_type=jnp.float32
        ).astype(jnp.bfloat16)


def own_block(shape, channels):
    row = lax.broadcasted_iota(jnp.int32, shape, 0)
    return lanes_of(shape) // channels == row % 8


def mixed_forward(coeffs, weights, mixed):
    count, width = coeffs.shape
    channels = width // 2
    mine = own_block((8, 8 * channels), channels)
    low = lanes_of((8, width)) < channels
    for start in range(0, count, 8):
        pair = coeffs[start : start + 8].astype(jnp.float32)
        swapped = halves_swapped(pair)
        real = jnp.where(low, pair, swapped)
        imag = jnp.where(low, swapped, pair)
        spread = jnp.concatenate(
            [jnp.where(mine, jnp.concatenate([part] * 4, 1), 0.0) for part in (real, imag)], 0
        ).astype(jnp.bfloat16)
        both = dot(spread, weights[pl.ds(start * channels, 8 * channels), :])
        mixed[pl.ds(start, 8), :] = both[:8] + quarter_turn(both[8:], 1)


def mixed_backward(coeffs, weights, mixed):
    count, width = coeffs.shape
    channels = width // 2
    mine = own_block((8, 8 * channels), channels)
    low = lanes_of((8, width)) < channels
    for start in range(0, count, 8):
        pair = coeffs[start : start + 8].astype(jnp.float32)
        sides = jnp.concatenate([pair, quarter_turn(pair, -1)], 0).astype(jnp.bfloat16)
        every = lax.dot_general(
            sides,
            weights[pl.ds(start * channels, 8 * channels), :],
            (((1,), (1,)), ((), ())),
            preferred_element_type=jnp.float32,
        )
        folded = []
        for half in (every[:8], every[8:]):
            own = jnp.where(mine, half, 0.0)
            total = sum(own[:, at * width : (at + 1) * width] for at in range(4))
            folded.append(total + halves_swapped(total))
        mixed[pl.ds(start, 8), :] = jnp.where(low, folded[0], folded[1])


def mix_forward_kernel(norm_scale, mode_data, along_x, weights, coeffs_out, planes_out, mixed):
    coeffs = coeffs_of(along_x, mode_data, norm_scale)
    coeffs_out[...] = coeffs
    mixed_forward(coeffs, weights, mixed)
    store_planes(along_x, mixed, planes_out)


def mix_backward_kernel(
    norm_scale, samples, core, mode_data, along_x, weights, coeffs_in, kept, given, planes_out, mixed
):
    coeffs = coeffs_of(along_x, mode_data, norm_scale)
    first_core = core[0] == 0
    size = coeffs.shape[0] // samples
    for side, values in enumerate((coeffs_in[...], coeffs)):
        for place in range(samples // 2):
            even = values[2 * place * size : (2 * place + 1) * size].astype(jnp.float32)
            odd = values[(2 * place + 1) * size : (2 * place + 2) * size].astype(jnp.float32)
            rows = pl.ds((side * (samples // 2) + place) * size, size)
            kept[rows, :] = jnp.where(first_core, even, odd).astype(jnp.bfloat16)
            given[rows, :] = jnp.where(first_core, odd, even).astype(jnp.bfloat16)
    mixed_backward(coeffs, weights, mixed)
    store_planes(along_x, mixed, planes_out)


def call_first(operands, modes_shape, scratch):
    outs = [jax.ShapeDtypeStruct(modes_shape, jnp.bfloat16)] + [
        jax.ShapeDtypeStruct(array.shape, array.dtype) for array in operands
    ]
    return pl.pallas_call(
        forward_yz_kernel,
        name="forward_yz",
        out_shape=outs,
        in_specs=[pl.BlockSpec(memory_space=pltpu.HBM)] * len(operands),
        out_specs=[pl.BlockSpec(memory_space=pltpu.VMEM)] * len(outs),
        scratch_shapes=[pltpu.VMEM(shape, jnp.float32) for shape in scratch]
        + [pltpu.SemaphoreType.DMA((PIECES + len(operands),))],
        compiler_params=pltpu.CompilerParams(vmem_limit_bytes=FIRST_BYTES),
    )(*(pltpu.with_memory_space_constraint(array, pltpu.HBM) for array in operands))


def call(kernel, operands, outs, scratch, name, scalars=()):
    whole = pl.BlockSpec(memory_space=pltpu.VMEM)
    return pl.pallas_call(
        kernel,
        name=name,
        out_shape=[jax.ShapeDtypeStruct(shape, jnp.bfloat16) for shape in outs],
        in_specs=[pl.BlockSpec(memory_space=pltpu.SMEM)] * len(scalars) + [whole] * len(operands),
        out_specs=[whole] * len(outs),
        scratch_shapes=[pltpu.VMEM(shape, jnp.float32) for shape in scratch],
        compiler_params=pltpu.CompilerParams(vmem_limit_bytes=SMALL_BYTES),
    )(*scalars, *operands)


def exchange(rows):
    count = lax.axis_size("gx")
    slots = rows.reshape(count, rows.shape[0] // count, rows.shape[1])
    return lax.all_to_all(slots, "gx", split_axis=0, concat_axis=0, tiled=True).reshape(rows.shape)


def swap_samples(kept, given, mine):
    count = lax.axis_size("sa")
    width = kept.shape[1]
    taken = lax.ppermute(given, "sa", [(i, i ^ 1) for i in range(count)])
    pair = jnp.stack([kept, taken], 0).reshape(2, 2, count // 2, -1, width)
    place = jnp.right_shift(mine, 1)
    arrived = [lax.dynamic_index_in_dim(pair, place, 2, keepdims=False)]
    for step in range(1, count // 2):
        block = lax.dynamic_index_in_dim(pair, jnp.bitwise_xor(place, step), 2, keepdims=False)
        arrived.append(lax.ppermute(block, "sa", [(i, i ^ 2 * step) for i in range(count)]))
    return jnp.concatenate(arrived, 0)


def sample_sum(left_side, right_side):
    samples, kx_count, mode_block, width = left_side.shape
    channels = width // 2
    left = left_side.reshape(samples, kx_count, mode_block, 2, channels)
    swapped = jnp.concatenate([right_side[..., channels:], -right_side[..., :channels]], -1)
    right = jnp.stack([right_side, swapped], 3)
    return jnp.einsum("skmtc,skmtp->kmcp", left, right, preferred_element_type=jnp.float32)


def on_device(field_in, cotangent, mode_weights, point_weights):
    field = field_in.reshape(field_in.shape[-2:])
    cotangent_rows = cotangent.reshape(field.shape)
    y_count, last_width = field.shape
    channels = point_weights.shape[0]
    kx_count, mode_block = mode_weights.shape[:2]
    x_length = lax.axis_size("gx")
    samples = lax.axis_size("sa")
    z_count = last_width // channels
    norm_scale = 1.0 / math.sqrt(x_length * y_count * z_count)
    width = 2 * channels
    mode_total = KY * KZ
    table_y = forward_table_y(y_count)
    inverse_y = inverse_table_y(y_count)
    along_x = table_x(kx_count, x_length, mode_block)
    table_y, inverse_y, along_x = map(jnp.asarray, (table_y, inverse_y, along_x))
    weights = mode_weights.reshape(-1, width)
    scaled = lambda kernel: lambda *refs: kernel(norm_scale, *refs)
    rows = kx_count * mode_block
    planar = (mode_total, width)
    stacked = (2 * KY, last_width)
    mine = lax.axis_index("sa")
    core, field = lax.optimization_barrier((jnp.bitwise_and(mine, 1).reshape(1), field))

    modes, field, table_y, weights, along_x, inverse_y, point_weights, cotangent_rows = call_first(
        (field, table_y, weights, along_x, inverse_y, point_weights, cotangent_rows), planar, [stacked, planar]
    )
    coeffs_in, planes = call(
        scaled(mix_forward_kernel),
        (exchange(modes), along_x, weights),
        [(rows, width), planar],
        [(rows, width)],
        "mix_forward",
    )
    modes, field_out, out_grad = call(
        scaled(middle_kernel),
        (exchange(planes), inverse_y, table_y, point_weights, field, cotangent_rows),
        [planar, field.shape, field.shape],
        [stacked, stacked, planar],
        "middle",
    )
    kept, given, planes = call(
        lambda *refs: mix_backward_kernel(norm_scale, samples, *refs),
        (exchange(modes), along_x, weights, coeffs_in),
        [(rows, width), (rows, width), planar],
        [(rows, width)],
        "mix_backward",
        (core,),
    )
    shared = swap_samples(kept, given, mine).reshape(
        samples, 2, kx_count // samples, mode_block, width
    )
    (field_grad,) = call(
        scaled(last_kernel),
        (exchange(planes), inverse_y, point_weights, out_grad),
        [field.shape],
        [stacked, planar],
        "last",
    )
    shared, field_grad = lax.optimization_barrier((shared, field_grad))
    weight_grad = sample_sum(shared[:, 0], shared[:, 1])
    return (
        field_out.reshape(field_in.shape),
        field_grad.reshape(field_in.shape),
        weight_grad,
    )


def solution(mesh):
    in_specs = (
        P("sa", "gx", None, None),
        P("sa", "gx", None, None),
        P(None, "gx", None, None),
        P(),
    )
    out_specs = (P("sa", "gx", None, None), P("sa", "gx", None, None), P("sa", "gx", None, None))
    return jax.shard_map(
        on_device, mesh=mesh, in_specs=in_specs, out_specs=out_specs, check_vma=False
    )
```

```python
import math

import jax
import jax.numpy as jnp
import numpy as np
from jax import lax
from jax.experimental import pallas as pl
from jax.experimental.pallas import tpu as pltpu
from jax.sharding import PartitionSpec as P

KY = 32
KZ = 16
GELU_COEF = 0.044715
FIRST_BYTES = 16 << 20
SMALL_BYTES = 16 << 20
PIECES = 4
SORT_HINT = 40_000_000_000


def angles(freq_count, grid_count):
    frequency = np.arange(freq_count) - freq_count // 2
    turn_index = np.mod(frequency[:, None] * np.arange(grid_count)[None, :], grid_count)
    return turn_index.astype(np.float32) * np.float32(2.0 * math.pi / grid_count)


def tables_y(y_count):
    theta = angles(KY, y_count)
    return np.concatenate([np.cos(theta), -np.sin(theta)], 0).astype(np.float32)


def forward_table_y(y_count):
    return tables_y(y_count).astype(jnp.bfloat16)


def inverse_table_y(y_count):
    table = tables_y(y_count).T
    high = table.astype(jnp.bfloat16)
    low = (table - high.astype(np.float32)).astype(jnp.bfloat16)
    return np.concatenate([high, high, low], 1)


def table_x(kx_count, x_length, mode_block):
    theta = angles(kx_count, x_length)
    same = np.eye(mode_block, dtype=np.float32)
    cos_wide = np.kron(np.cos(theta), same)
    sin_wide = np.kron(np.sin(theta), same)
    return np.concatenate([cos_wide, sin_wide], 0).astype(jnp.bfloat16)


def dot(left, right):
    return jnp.dot(left, right, preferred_element_type=jnp.float32)


def lanes_of(shape):
    return lax.broadcasted_iota(jnp.int32, shape, 1)


def halves_swapped(pair):
    return pltpu.roll(pair, pair.shape[1] // 2, 1)


def quarter_turn(pair, sign):
    low = lanes_of(pair.shape) < pair.shape[1] // 2
    swapped = halves_swapped(pair)
    return jnp.where(low, -swapped, swapped) if sign > 0 else jnp.where(low, swapped, -swapped)


def fourier(parts, sign):
    count = len(parts)
    if count == 1:
        return parts
    even = fourier(parts[0::2], sign)
    odd = fourier(parts[1::2], sign)
    lower, upper = [], []
    for k in range(count // 2):
        turned = odd[k]
        if 4 * k == count:
            turned = quarter_turn(turned, sign)
        elif k:
            angle = 2.0 * math.pi * k / count
            turned = math.cos(angle) * turned + math.sin(angle) * quarter_turn(turned, sign)
        lower.append(even[k] + turned)
        upper.append(even[k] - turned)
    return lower + upper


class Fetched:
    def __init__(self, source, target, semaphores, first, pieces=1, axis=0):
        size = source.shape[axis] // pieces
        self.copies = []
        for at in range(pieces):
            part = pl.ds(at * size, size)
            index = (part,) if axis == 0 else (slice(None), part)
            self.copies.append(
                pltpu.make_async_copy(source.at[index], target.at[index], semaphores.at[first + at])
            )

    def start(self, at=None):
        for copy in self.copies if at is None else self.copies[at : at + 1]:
            copy.start()

    def wait(self, at=None):
        for copy in self.copies if at is None else self.copies[at : at + 1]:
            copy.wait()


def modes_from(first_pass, wide_modes, modes_out):
    width = modes_out.shape[1]
    low = lanes_of((8, width)) < width // 2
    for block in range(KY // 8):
        parts = []
        for column in range(KZ // 2):
            lanes = pl.ds(column * width, width)
            real = first_pass[pl.ds(block * 8, 8), lanes]
            imag = first_pass[pl.ds(KY + block * 8, 8), lanes]
            parts.append(jnp.where(low, real, halves_swapped(imag)))
            parts.append(jnp.where(low, halves_swapped(real), imag))
        spectrum = fourier(parts, -1)
        for kz in range(KZ):
            wide_modes[pl.ds(block * 8 * KZ + kz, 8, stride=KZ), :] = spectrum[(kz + KZ // 2) % KZ]
        rows = pl.ds(block * 8 * KZ, 8 * KZ)
        modes_out[rows, :] = wide_modes[rows, :].astype(modes_out.dtype)


def stacked_from(planes, wide_modes, stacked, norm_scale):
    width = planes.shape[1]
    low = lanes_of((8, width)) < width // 2
    wide_modes[...] = planes[...].astype(jnp.float32)
    for block in range(KY // 8):
        parts = [
            wide_modes[pl.ds(block * 8 * KZ + (k + KZ // 2) % KZ, 8, stride=KZ), :] for k in range(KZ)
        ]
        grid = fourier(parts, 1)
        for column in range(KZ // 2):
            lanes = pl.ds(column * width, width)
            first = grid[2 * column] * norm_scale
            second = grid[2 * column + 1] * norm_scale
            stacked[pl.ds(block * 8, 8), lanes] = jnp.where(low, first, halves_swapped(second))
            stacked[pl.ds(KY + block * 8, 8), lanes] = jnp.where(low, halves_swapped(first), second)


def three_terms(stacked, lanes):
    value = stacked[:, lanes]
    high = value.astype(jnp.bfloat16)
    low = (value - high.astype(jnp.float32)).astype(jnp.bfloat16)
    return jnp.concatenate([high, low, high], 0)


def paired_of(point_weights):
    channels = point_weights.shape[0]
    wide = jnp.concatenate([point_weights[...].astype(jnp.float32)] * 4, 1)
    tall = jnp.concatenate([wide] * 4, 0)
    row = lax.broadcasted_iota(jnp.int32, tall.shape, 0)
    return jnp.where(row // channels == lanes_of(tall.shape) // channels, tall, 0.0).astype(jnp.bfloat16)


def forward_yz_kernel(*refs):
    count = (len(refs) - 4) // 2
    sources, (modes_out, *targets) = refs[:count], refs[count : 2 * count + 1]
    first_pass, wide_modes, semaphores = refs[2 * count + 1 :]
    fetches = [
        Fetched(source, target, semaphores, at, PIECES if at == 0 else 1, 1)
        if at == 0
        else Fetched(source, target, semaphores, PIECES + at)
        for at, (source, target) in enumerate(zip(sources, targets))
    ]
    fetches[1].start()
    fetches[0].start()
    for fetch in fetches[2:]:
        fetch.start()
    field, table_y = targets[:2]
    fetches[1].wait()
    width = field.shape[1] // PIECES
    for column in range(PIECES):
        lanes = pl.ds(column * width, width)
        fetches[0].wait(column)
        first_pass[:, lanes] = dot(table_y[...], field[:, lanes])
    modes_from(first_pass, wide_modes, modes_out)
    for fetch in fetches[2:]:
        fetch.wait()


def middle_kernel(
    norm_scale, planes, inverse_y, table_y, point_weights, field, cotangent,
    modes_out, field_out_hbm, out_grad, stacked, first_pass, wide_modes, field_out, semaphores,
):
    store = Fetched(field_out, field_out_hbm, semaphores, 0, PIECES, 1)
    paired = paired_of(point_weights)
    stacked_from(planes, wide_modes, stacked, norm_scale)
    root_const = math.sqrt(2.0 / math.pi)
    width = field.shape[1] // PIECES
    rows_per = 64
    for column in range(PIECES):
        lanes = pl.ds(column * width, width)
        terms = three_terms(stacked, lanes)
        for start in range(0, field.shape[0], rows_per):
            rows = pl.ds(start, rows_per)
            pre_act = dot(inverse_y[rows, :], terms) + dot(field[rows, lanes], paired)
            square = pre_act * pre_act
            tangent = jnp.tanh(pre_act * (root_const + root_const * GELU_COEF * square))
            half = 0.5 + 0.5 * tangent
            activated = pre_act * half
            slope = half + activated * (1.0 - tangent) * (root_const + 3.0 * root_const * GELU_COEF * square)
            field_out[rows, lanes] = activated.astype(field_out.dtype)
            out_grad[rows, lanes] = (cotangent[rows, lanes].astype(jnp.float32) * slope).astype(out_grad.dtype)
        store.start(column)
        first_pass[:, lanes] = dot(table_y[...], out_grad[:, lanes])
    modes_from(first_pass, wide_modes, modes_out)
    store.wait()


def last_kernel(
    norm_scale, planes, inverse_y, point_weights, out_grad,
    field_grad_hbm, stacked, wide_modes, field_grad, semaphores,
):
    store = Fetched(field_grad, field_grad_hbm, semaphores, 0, PIECES, 1)
    paired = paired_of(point_weights)
    stacked_from(planes, wide_modes, stacked, norm_scale)
    width = paired.shape[0]
    rows_per = 128
    for column in range(PIECES):
        lanes = pl.ds(column * width, width)
        terms = three_terms(stacked, lanes)
        for start in range(0, out_grad.shape[0], rows_per):
            rows = pl.ds(start, rows_per)
            mixed = lax.dot_general(
                out_grad[rows, lanes], paired, (((1,), (1,)), ((), ())), preferred_element_type=jnp.float32
            )
            field_grad[rows, lanes] = (dot(inverse_y[rows, :], terms) + mixed).astype(field_grad.dtype)
        store.start(column)
    store.wait()


def coeffs_of(along_x, mode_data, norm_scale):
    both = dot(along_x[...], mode_data[...])
    count = both.shape[0] // 2
    return ((both[:count] + quarter_turn(both[count:], -1)) * norm_scale).astype(jnp.bfloat16)


def store_planes(along_x, mixed, planes_out):
    mixed = mixed[...]
    turned = quarter_turn(mixed.astype(jnp.bfloat16).astype(jnp.float32), 1).astype(jnp.bfloat16)
    terms = jnp.concatenate([mixed.astype(jnp.bfloat16), turned], 0)
    size = planes_out.shape[0] // PIECES
    for piece in range(PIECES):
        rows = pl.ds(piece * size, size)
        planes_out[rows, :] = lax.dot_general(
            along_x[:, rows], terms, (((0,), (0,)), ((), ())), preferred_element_type=jnp.float32
        ).astype(jnp.bfloat16)


def own_block(shape, channels):
    row = lax.broadcasted_iota(jnp.int32, shape, 0)
    return lanes_of(shape) // channels == row % 8


def mixed_forward(coeffs, weights, mixed):
    count, width = coeffs.shape
    channels = width // 2
    mine = own_block((8, 8 * channels), channels)
    low = lanes_of((8, width)) < channels
    for start in range(0, count, 8):
        pair = coeffs[start : start + 8].astype(jnp.float32)
        swapped = halves_swapped(pair)
        real = jnp.where(low, pair, swapped)
        imag = jnp.where(low, swapped, pair)
        spread = jnp.concatenate(
            [jnp.where(mine, jnp.concatenate([part] * 4, 1), 0.0) for part in (real, imag)], 0
        ).astype(jnp.bfloat16)
        both = dot(spread, weights[pl.ds(start * channels, 8 * channels), :])
        mixed[pl.ds(start, 8), :] = both[:8] + quarter_turn(both[8:], 1)


def mixed_backward(coeffs, weights, mixed):
    count, width = coeffs.shape
    channels = width // 2
    mine = own_block((8, 8 * channels), channels)
    low = lanes_of((8, width)) < channels
    for start in range(0, count, 8):
        pair = coeffs[start : start + 8].astype(jnp.float32)
        sides = jnp.concatenate([pair, quarter_turn(pair, -1)], 0).astype(jnp.bfloat16)
        every = lax.dot_general(
            sides,
            weights[pl.ds(start * channels, 8 * channels), :],
            (((1,), (1,)), ((), ())),
            preferred_element_type=jnp.float32,
        )
        folded = []
        for half in (every[:8], every[8:]):
            own = jnp.where(mine, half, 0.0)
            total = sum(own[:, at * width : (at + 1) * width] for at in range(4))
            folded.append(total + halves_swapped(total))
        mixed[pl.ds(start, 8), :] = jnp.where(low, folded[0], folded[1])


def mix_forward_kernel(norm_scale, mode_data, along_x, weights, coeffs_out, planes_out, mixed):
    coeffs = coeffs_of(along_x, mode_data, norm_scale)
    coeffs_out[...] = coeffs
    mixed_forward(coeffs, weights, mixed)
    store_planes(along_x, mixed, planes_out)


def mix_backward_kernel(
    norm_scale, samples, core, mode_data, along_x, weights, coeffs_in, kept, given, planes_out, mixed
):
    coeffs = coeffs_of(along_x, mode_data, norm_scale)
    first_core = core[0] == 0
    size = coeffs.shape[0] // samples
    for side, values in enumerate((coeffs_in[...], coeffs)):
        for place in range(samples // 2):
            even = values[2 * place * size : (2 * place + 1) * size].astype(jnp.float32)
            odd = values[(2 * place + 1) * size : (2 * place + 2) * size].astype(jnp.float32)
            rows = pl.ds((side * (samples // 2) + place) * size, size)
            kept[rows, :] = jnp.where(first_core, even, odd).astype(jnp.bfloat16)
            given[rows, :] = jnp.where(first_core, odd, even).astype(jnp.bfloat16)
    mixed_backward(coeffs, weights, mixed)
    store_planes(along_x, mixed, planes_out)


def call_first(operands, modes_shape, scratch):
    outs = [jax.ShapeDtypeStruct(modes_shape, jnp.bfloat16)] + [
        jax.ShapeDtypeStruct(array.shape, array.dtype) for array in operands
    ]
    return pl.pallas_call(
        forward_yz_kernel,
        name="forward_yz",
        out_shape=outs,
        in_specs=[pl.BlockSpec(memory_space=pltpu.HBM)] * len(operands),
        out_specs=[pl.BlockSpec(memory_space=pltpu.VMEM)] * len(outs),
        scratch_shapes=[pltpu.VMEM(shape, jnp.float32) for shape in scratch]
        + [pltpu.SemaphoreType.DMA((PIECES + len(operands),))],
        compiler_params=pltpu.CompilerParams(vmem_limit_bytes=FIRST_BYTES),
    )(*(pltpu.with_memory_space_constraint(array, pltpu.HBM) for array in operands))


def call(kernel, operands, outs, scratch, name, scalars=(), estimate=None, stored=None):
    whole = pl.BlockSpec(memory_space=pltpu.VMEM)
    out_specs = [whole] * len(outs)
    scratch_shapes = [pltpu.VMEM(shape, jnp.float32) for shape in scratch]
    if stored is not None:
        out_specs[stored] = pl.BlockSpec(memory_space=pl.ANY)
        scratch_shapes += [pltpu.VMEM(outs[stored], jnp.bfloat16), pltpu.SemaphoreType.DMA((PIECES,))]
    return pl.pallas_call(
        kernel,
        name=name,
        cost_estimate=estimate,
        out_shape=[jax.ShapeDtypeStruct(shape, jnp.bfloat16) for shape in outs],
        in_specs=[pl.BlockSpec(memory_space=pltpu.SMEM)] * len(scalars) + [whole] * len(operands),
        out_specs=out_specs,
        scratch_shapes=scratch_shapes,
        compiler_params=pltpu.CompilerParams(vmem_limit_bytes=SMALL_BYTES),
    )(*scalars, *operands)


def exchange(rows):
    count = lax.axis_size("gx")
    slots = rows.reshape(count, rows.shape[0] // count, rows.shape[1])
    return lax.all_to_all(slots, "gx", split_axis=0, concat_axis=0, tiled=True).reshape(rows.shape)


def sort_kernel(place, kept, taken, *blocks):
    size = kept.shape[0] // (2 * len(blocks))
    for step, block in enumerate(blocks):
        wanted = jnp.bitwise_xor(place[0], step)
        for core, source in enumerate((kept, taken)):
            for side in range(2):
                start = pl.multiple_of((side * len(blocks) + wanted) * size, size)
                block[pl.ds((2 * core + side) * size, size), :] = source[pl.ds(start, size), :]


def swap_samples(kept, given, place):
    count = lax.axis_size("sa")
    taken = lax.ppermute(given, "sa", [(i, i ^ 1) for i in range(count)])
    rows, width = kept.shape
    blocks = call(
        sort_kernel,
        (kept, taken),
        [(4 * rows // count, width)] * (count // 2),
        [],
        "sort",
        (place,),
        pl.CostEstimate(flops=SORT_HINT, bytes_accessed=4 * rows * width, transcendentals=0),
    )
    return [blocks[0]] + [
        lax.ppermute(blocks[step], "sa", [(i, i ^ 2 * step) for i in range(count)])
        for step in range(1, count // 2)
    ]


def sample_sum(left_side, right_side):
    samples, kx_count, mode_block, width = left_side.shape
    channels = width // 2
    left = left_side.reshape(samples, kx_count, mode_block, 2, channels)
    swapped = jnp.concatenate([right_side[..., channels:], -right_side[..., :channels]], -1)
    right = jnp.stack([right_side, swapped], 3)
    return jnp.einsum("skmtc,skmtp->kmcp", left, right, preferred_element_type=jnp.float32)


def on_device(field_in, cotangent, mode_weights, point_weights):
    field = field_in.reshape(field_in.shape[-2:])
    cotangent_rows = cotangent.reshape(field.shape)
    y_count, last_width = field.shape
    channels = point_weights.shape[0]
    kx_count, mode_block = mode_weights.shape[:2]
    x_length = lax.axis_size("gx")
    samples = lax.axis_size("sa")
    z_count = last_width // channels
    norm_scale = 1.0 / math.sqrt(x_length * y_count * z_count)
    width = 2 * channels
    mode_total = KY * KZ
    table_y = forward_table_y(y_count)
    inverse_y = inverse_table_y(y_count)
    along_x = table_x(kx_count, x_length, mode_block)
    table_y, inverse_y, along_x = map(jnp.asarray, (table_y, inverse_y, along_x))
    weights = mode_weights.reshape(-1, width)
    scaled = lambda kernel: lambda *refs: kernel(norm_scale, *refs)
    rows = kx_count * mode_block
    planar = (mode_total, width)
    stacked = (2 * KY, last_width)
    mine = lax.axis_index("sa")
    core, place, field = lax.optimization_barrier(
        (jnp.bitwise_and(mine, 1).reshape(1), jnp.right_shift(mine, 1).reshape(1), field)
    )

    modes, field, table_y, weights, along_x, inverse_y, point_weights, cotangent_rows = call_first(
        (field, table_y, weights, along_x, inverse_y, point_weights, cotangent_rows), planar, [stacked, planar]
    )
    coeffs_in, planes = call(
        scaled(mix_forward_kernel),
        (exchange(modes), along_x, weights),
        [(rows, width), planar],
        [(rows, width)],
        "mix_forward",
    )
    modes, field_out, out_grad = call(
        scaled(middle_kernel),
        (exchange(planes), inverse_y, table_y, point_weights, field, cotangent_rows),
        [planar, field.shape, field.shape],
        [stacked, stacked, planar],
        "middle",
        stored=1,
    )
    kept, given, planes = call(
        lambda *refs: mix_backward_kernel(norm_scale, samples, *refs),
        (exchange(modes), along_x, weights, coeffs_in),
        [(rows, width), (rows, width), planar],
        [(rows, width)],
        "mix_backward",
        (core,),
    )
    arrived = swap_samples(kept, given, place)
    (field_grad,) = call(
        scaled(last_kernel),
        (exchange(planes), inverse_y, point_weights, out_grad),
        [field.shape],
        [stacked, planar],
        "last",
        stored=0,
    )
    arrived, field_grad = lax.optimization_barrier((arrived, field_grad))
    shared = jnp.concatenate(arrived, 0).reshape(samples, 2, kx_count // samples, mode_block, width)
    weight_grad = sample_sum(shared[:, 0], shared[:, 1])
    return (
        field_out.reshape(field_in.shape),
        field_grad.reshape(field_in.shape),
        weight_grad,
    )


def solution(mesh):
    in_specs = (
        P("sa", "gx", None, None),
        P("sa", "gx", None, None),
        P(None, "gx", None, None),
        P(),
    )
    out_specs = (P("sa", "gx", None, None), P("sa", "gx", None, None), P("sa", "gx", None, None))
    return jax.shard_map(
        on_device, mesh=mesh, in_specs=in_specs, out_specs=out_specs, check_vma=False
    )
```

```python
import math

import jax
import jax.numpy as jnp
import numpy as np
from jax import lax
from jax.experimental import pallas as pl
from jax.experimental.pallas import tpu as pltpu
from jax.sharding import PartitionSpec as P

KY = 32
KZ = 16
GELU_COEF = 0.044715
FIRST_BYTES = 16 << 20
SMALL_BYTES = 16 << 20
PIECES = 4
SORT_HINT = 40_000_000_000


def angles(freq_count, grid_count):
    frequency = np.arange(freq_count) - freq_count // 2
    turn_index = np.mod(frequency[:, None] * np.arange(grid_count)[None, :], grid_count)
    return turn_index.astype(np.float32) * np.float32(2.0 * math.pi / grid_count)


def tables_y(y_count):
    theta = angles(KY, y_count)
    return np.concatenate([np.cos(theta), -np.sin(theta)], 0).astype(np.float32)


def forward_table_y(y_count):
    return tables_y(y_count).astype(jnp.bfloat16)


def inverse_table_y(y_count):
    table = tables_y(y_count).T
    high = table.astype(jnp.bfloat16)
    low = (table - high.astype(np.float32)).astype(jnp.bfloat16)
    return np.concatenate([high, high, low], 1)


def table_x(kx_count, x_length, mode_block):
    theta = angles(kx_count, x_length)
    same = np.eye(mode_block, dtype=np.float32)
    cos_wide = np.kron(np.cos(theta), same)
    sin_wide = np.kron(np.sin(theta), same)
    return np.concatenate([cos_wide, sin_wide], 0).astype(jnp.bfloat16)


def dot(left, right):
    return jnp.dot(left, right, preferred_element_type=jnp.float32)


def lanes_of(shape):
    return lax.broadcasted_iota(jnp.int32, shape, 1)


def halves_swapped(pair):
    return pltpu.roll(pair, pair.shape[1] // 2, 1)


def quarter_turn(pair, sign):
    low = lanes_of(pair.shape) < pair.shape[1] // 2
    swapped = halves_swapped(pair)
    return jnp.where(low, -swapped, swapped) if sign > 0 else jnp.where(low, swapped, -swapped)


def fourier(parts, sign):
    count = len(parts)
    if count == 1:
        return parts
    even = fourier(parts[0::2], sign)
    odd = fourier(parts[1::2], sign)
    lower, upper = [], []
    for k in range(count // 2):
        turned = odd[k]
        if 4 * k == count:
            turned = quarter_turn(turned, sign)
        elif k:
            angle = 2.0 * math.pi * k / count
            turned = math.cos(angle) * turned + math.sin(angle) * quarter_turn(turned, sign)
        lower.append(even[k] + turned)
        upper.append(even[k] - turned)
    return lower + upper


class Fetched:
    def __init__(self, source, target, semaphores, first, pieces=1, axis=0):
        size = source.shape[axis] // pieces
        self.copies = []
        for at in range(pieces):
            part = pl.ds(at * size, size)
            index = (part,) if axis == 0 else (slice(None), part)
            self.copies.append(
                pltpu.make_async_copy(source.at[index], target.at[index], semaphores.at[first + at])
            )

    def start(self, at=None):
        for copy in self.copies if at is None else self.copies[at : at + 1]:
            copy.start()

    def wait(self, at=None):
        for copy in self.copies if at is None else self.copies[at : at + 1]:
            copy.wait()


def modes_from(first_pass, wide_modes, modes_out):
    width = modes_out.shape[1]
    low = lanes_of((8, width)) < width // 2
    for block in range(KY // 8):
        parts = []
        for column in range(KZ // 2):
            lanes = pl.ds(column * width, width)
            real = first_pass[pl.ds(block * 8, 8), lanes]
            imag = first_pass[pl.ds(KY + block * 8, 8), lanes]
            parts.append(jnp.where(low, real, halves_swapped(imag)))
            parts.append(jnp.where(low, halves_swapped(real), imag))
        spectrum = fourier(parts, -1)
        for kz in range(KZ):
            wide_modes[pl.ds(block * 8 * KZ + kz, 8, stride=KZ), :] = spectrum[(kz + KZ // 2) % KZ]
        rows = pl.ds(block * 8 * KZ, 8 * KZ)
        modes_out[rows, :] = wide_modes[rows, :].astype(modes_out.dtype)


def stacked_from(planes, wide_modes, stacked, norm_scale):
    width = planes.shape[1]
    low = lanes_of((8, width)) < width // 2
    wide_modes[...] = planes[...].astype(jnp.float32)
    for block in range(KY // 8):
        parts = [
            wide_modes[pl.ds(block * 8 * KZ + (k + KZ // 2) % KZ, 8, stride=KZ), :] for k in range(KZ)
        ]
        grid = fourier(parts, 1)
        for column in range(KZ // 2):
            lanes = pl.ds(column * width, width)
            first = grid[2 * column] * norm_scale
            second = grid[2 * column + 1] * norm_scale
            stacked[pl.ds(block * 8, 8), lanes] = jnp.where(low, first, halves_swapped(second))
            stacked[pl.ds(KY + block * 8, 8), lanes] = jnp.where(low, halves_swapped(first), second)


def three_terms(stacked, lanes):
    value = stacked[:, lanes]
    high = value.astype(jnp.bfloat16)
    low = (value - high.astype(jnp.float32)).astype(jnp.bfloat16)
    return jnp.concatenate([high, low, high], 0)


def paired_of(point_weights):
    channels = point_weights.shape[0]
    wide = jnp.concatenate([point_weights[...].astype(jnp.float32)] * 4, 1)
    tall = jnp.concatenate([wide] * 4, 0)
    row = lax.broadcasted_iota(jnp.int32, tall.shape, 0)
    return jnp.where(row // channels == lanes_of(tall.shape) // channels, tall, 0.0).astype(jnp.bfloat16)


def forward_yz_kernel(*refs):
    count = (len(refs) - 4) // 2
    sources, (modes_out, *targets) = refs[:count], refs[count : 2 * count + 1]
    first_pass, wide_modes, semaphores = refs[2 * count + 1 :]
    fetches = [
        Fetched(source, target, semaphores, at, PIECES if at == 0 else 1, 1)
        if at == 0
        else Fetched(source, target, semaphores, PIECES + at)
        for at, (source, target) in enumerate(zip(sources, targets))
    ]
    fetches[1].start()
    fetches[0].start()
    for fetch in fetches[2:]:
        fetch.start()
    field, table_y = targets[:2]
    fetches[1].wait()
    width = field.shape[1] // PIECES
    for column in range(PIECES):
        lanes = pl.ds(column * width, width)
        fetches[0].wait(column)
        first_pass[:, lanes] = dot(table_y[...], field[:, lanes])
    modes_from(first_pass, wide_modes, modes_out)
    for fetch in fetches[2:]:
        fetch.wait()


def middle_kernel(
    norm_scale, planes, inverse_y, table_y, point_weights, field, cotangent,
    modes_out, field_out_hbm, out_grad, stacked, first_pass, wide_modes, field_out, semaphores,
):
    store = Fetched(field_out, field_out_hbm, semaphores, 0, PIECES, 1)
    paired = paired_of(point_weights)
    stacked_from(planes, wide_modes, stacked, norm_scale)
    root_const = math.sqrt(2.0 / math.pi)
    width = field.shape[1] // PIECES
    rows_per = 64
    for column in range(PIECES):
        lanes = pl.ds(column * width, width)
        terms = three_terms(stacked, lanes)
        for start in range(0, field.shape[0], rows_per):
            rows = pl.ds(start, rows_per)
            pre_act = dot(inverse_y[rows, :], terms) + dot(field[rows, lanes], paired)
            square = pre_act * pre_act
            tangent = jnp.tanh(pre_act * (root_const + root_const * GELU_COEF * square))
            half = 0.5 + 0.5 * tangent
            activated = pre_act * half
            slope = half + activated * (1.0 - tangent) * (root_const + 3.0 * root_const * GELU_COEF * square)
            field_out[rows, lanes] = activated.astype(field_out.dtype)
            out_grad[rows, lanes] = (cotangent[rows, lanes].astype(jnp.float32) * slope).astype(out_grad.dtype)
        store.start(column)
        first_pass[:, lanes] = dot(table_y[...], out_grad[:, lanes])
    modes_from(first_pass, wide_modes, modes_out)
    store.wait()


def last_kernel(
    norm_scale, planes, inverse_y, point_weights, out_grad,
    field_grad_hbm, stacked, wide_modes, field_grad, semaphores,
):
    store = Fetched(field_grad, field_grad_hbm, semaphores, 0, PIECES, 1)
    paired = paired_of(point_weights)
    stacked_from(planes, wide_modes, stacked, norm_scale)
    width = paired.shape[0]
    rows_per = 128
    for column in range(PIECES):
        lanes = pl.ds(column * width, width)
        terms = three_terms(stacked, lanes)
        for start in range(0, out_grad.shape[0], rows_per):
            rows = pl.ds(start, rows_per)
            mixed = lax.dot_general(
                out_grad[rows, lanes], paired, (((1,), (1,)), ((), ())), preferred_element_type=jnp.float32
            )
            field_grad[rows, lanes] = (dot(inverse_y[rows, :], terms) + mixed).astype(field_grad.dtype)
        store.start(column)
    store.wait()


def coeffs_of(along_x, mode_data, norm_scale):
    both = dot(along_x[...], mode_data[...])
    count = both.shape[0] // 2
    return ((both[:count] + quarter_turn(both[count:], -1)) * norm_scale).astype(jnp.bfloat16)


def store_planes(along_x, mixed, planes_out, store=None):
    mixed = mixed[...]
    turned = quarter_turn(mixed.astype(jnp.bfloat16).astype(jnp.float32), 1).astype(jnp.bfloat16)
    terms = jnp.concatenate([mixed.astype(jnp.bfloat16), turned], 0)
    size = planes_out.shape[0] // PIECES
    for piece in range(PIECES):
        rows = pl.ds(piece * size, size)
        planes_out[rows, :] = lax.dot_general(
            along_x[:, rows], terms, (((0,), (0,)), ((), ())), preferred_element_type=jnp.float32
        ).astype(jnp.bfloat16)
        if store is not None:
            store.start(piece)
    if store is not None:
        store.wait()


def own_block(shape, channels):
    row = lax.broadcasted_iota(jnp.int32, shape, 0)
    return lanes_of(shape) // channels == row % 8


def mixed_forward(coeffs, weights, mixed):
    count, width = coeffs.shape
    channels = width // 2
    mine = own_block((8, 8 * channels), channels)
    low = lanes_of((8, width)) < channels
    for start in range(0, count, 8):
        pair = coeffs[start : start + 8].astype(jnp.float32)
        swapped = halves_swapped(pair)
        real = jnp.where(low, pair, swapped)
        imag = jnp.where(low, swapped, pair)
        spread = jnp.concatenate(
            [jnp.where(mine, jnp.concatenate([part] * 4, 1), 0.0) for part in (real, imag)], 0
        ).astype(jnp.bfloat16)
        both = dot(spread, weights[pl.ds(start * channels, 8 * channels), :])
        mixed[pl.ds(start, 8), :] = both[:8] + quarter_turn(both[8:], 1)


def mixed_backward(coeffs, weights, mixed):
    count, width = coeffs.shape
    channels = width // 2
    mine = own_block((8, 8 * channels), channels)
    low = lanes_of((8, width)) < channels
    for start in range(0, count, 8):
        pair = coeffs[start : start + 8].astype(jnp.float32)
        sides = jnp.concatenate([pair, quarter_turn(pair, -1)], 0).astype(jnp.bfloat16)
        every = lax.dot_general(
            sides,
            weights[pl.ds(start * channels, 8 * channels), :],
            (((1,), (1,)), ((), ())),
            preferred_element_type=jnp.float32,
        )
        folded = []
        for half in (every[:8], every[8:]):
            own = jnp.where(mine, half, 0.0)
            total = sum(own[:, at * width : (at + 1) * width] for at in range(4))
            folded.append(total + halves_swapped(total))
        mixed[pl.ds(start, 8), :] = jnp.where(low, folded[0], folded[1])


def mix_forward_kernel(
    norm_scale, mode_data, along_x, weights, later_hbm, coeffs_out, planes_out, later, mixed, semaphores
):
    fetch = Fetched(later_hbm, later, semaphores, 0)
    fetch.start()
    coeffs = coeffs_of(along_x, mode_data, norm_scale)
    coeffs_out[...] = coeffs
    mixed_forward(coeffs, weights, mixed)
    store_planes(along_x, mixed, planes_out)
    fetch.wait()


def mix_backward_kernel(
    norm_scale, samples, core, mode_data, along_x, weights, coeffs_in,
    kept, given, planes_hbm, mixed, planes_out, semaphores,
):
    store = Fetched(planes_out, planes_hbm, semaphores, 0, PIECES)
    coeffs = coeffs_of(along_x, mode_data, norm_scale)
    first_core = core[0] == 0
    size = coeffs.shape[0] // samples
    for side, values in enumerate((coeffs_in[...], coeffs)):
        for place in range(samples // 2):
            even = values[2 * place * size : (2 * place + 1) * size].astype(jnp.float32)
            odd = values[(2 * place + 1) * size : (2 * place + 2) * size].astype(jnp.float32)
            rows = pl.ds((side * (samples // 2) + place) * size, size)
            kept[rows, :] = jnp.where(first_core, even, odd).astype(jnp.bfloat16)
            given[rows, :] = jnp.where(first_core, odd, even).astype(jnp.bfloat16)
    mixed_backward(coeffs, weights, mixed)
    store_planes(along_x, mixed, planes_out, store)


def call_first(operands, modes_shape, scratch):
    outs = [jax.ShapeDtypeStruct(modes_shape, jnp.bfloat16)] + [
        jax.ShapeDtypeStruct(array.shape, array.dtype) for array in operands
    ]
    return pl.pallas_call(
        forward_yz_kernel,
        name="forward_yz",
        out_shape=outs,
        in_specs=[pl.BlockSpec(memory_space=pltpu.HBM)] * len(operands),
        out_specs=[pl.BlockSpec(memory_space=pltpu.VMEM)] * len(outs),
        scratch_shapes=[pltpu.VMEM(shape, jnp.float32) for shape in scratch]
        + [pltpu.SemaphoreType.DMA((PIECES + len(operands),))],
        compiler_params=pltpu.CompilerParams(vmem_limit_bytes=FIRST_BYTES),
    )(*(pltpu.with_memory_space_constraint(array, pltpu.HBM) for array in operands))


def call(kernel, operands, outs, scratch, name, scalars=(), estimate=None, stored=None, brought=None):
    whole = pl.BlockSpec(memory_space=pltpu.VMEM)
    out_specs = [whole] * len(outs)
    scratch_shapes = [pltpu.VMEM(shape, jnp.float32) for shape in scratch]
    if stored is not None:
        out_specs[stored] = pl.BlockSpec(memory_space=pl.ANY)
        scratch_shapes += [pltpu.VMEM(outs[stored], jnp.bfloat16), pltpu.SemaphoreType.DMA((PIECES,))]
    in_specs = [pl.BlockSpec(memory_space=pltpu.SMEM)] * len(scalars) + [whole] * len(operands)
    if brought is not None:
        operands = (*operands, pltpu.with_memory_space_constraint(brought, pltpu.HBM))
        in_specs.append(pl.BlockSpec(memory_space=pltpu.HBM))
        outs = [*outs, brought.shape]
        out_specs.append(whole)
        scratch_shapes.append(pltpu.SemaphoreType.DMA((1,)))
    return pl.pallas_call(
        kernel,
        name=name,
        cost_estimate=estimate,
        out_shape=[jax.ShapeDtypeStruct(shape, jnp.bfloat16) for shape in outs],
        in_specs=in_specs,
        out_specs=out_specs,
        scratch_shapes=scratch_shapes,
        compiler_params=pltpu.CompilerParams(vmem_limit_bytes=SMALL_BYTES),
    )(*scalars, *operands)


def exchange(rows):
    count = lax.axis_size("gx")
    slots = rows.reshape(count, rows.shape[0] // count, rows.shape[1])
    return lax.all_to_all(slots, "gx", split_axis=0, concat_axis=0, tiled=True).reshape(rows.shape)


def sort_kernel(place, kept, taken, *blocks):
    size = kept.shape[0] // (2 * len(blocks))
    for step, block in enumerate(blocks):
        wanted = jnp.bitwise_xor(place[0], step)
        for core, source in enumerate((kept, taken)):
            for side in range(2):
                start = pl.multiple_of((side * len(blocks) + wanted) * size, size)
                block[pl.ds((2 * core + side) * size, size), :] = source[pl.ds(start, size), :]


def swap_samples(kept, given, place):
    count = lax.axis_size("sa")
    taken = lax.ppermute(given, "sa", [(i, i ^ 1) for i in range(count)])
    rows, width = kept.shape
    blocks = call(
        sort_kernel,
        (kept, taken),
        [(4 * rows // count, width)] * (count // 2),
        [],
        "sort",
        (place,),
        pl.CostEstimate(flops=SORT_HINT, bytes_accessed=4 * rows * width, transcendentals=0),
    )
    return [blocks[0]] + [
        lax.ppermute(blocks[step], "sa", [(i, i ^ 2 * step) for i in range(count)])
        for step in range(1, count // 2)
    ]


def sample_sum(left_side, right_side):
    samples, kx_count, mode_block, width = left_side.shape
    channels = width // 2
    left = left_side.reshape(samples, kx_count, mode_block, 2, channels)
    swapped = jnp.concatenate([right_side[..., channels:], -right_side[..., :channels]], -1)
    right = jnp.stack([right_side, swapped], 3)
    return jnp.einsum("skmtc,skmtp->kmcp", left, right, preferred_element_type=jnp.float32)


def on_device(field_in, cotangent, mode_weights, point_weights):
    field = field_in.reshape(field_in.shape[-2:])
    cotangent_rows = cotangent.reshape(field.shape)
    y_count, last_width = field.shape
    channels = point_weights.shape[0]
    kx_count, mode_block = mode_weights.shape[:2]
    x_length = lax.axis_size("gx")
    samples = lax.axis_size("sa")
    z_count = last_width // channels
    norm_scale = 1.0 / math.sqrt(x_length * y_count * z_count)
    width = 2 * channels
    mode_total = KY * KZ
    table_y = forward_table_y(y_count)
    inverse_y = inverse_table_y(y_count)
    along_x = table_x(kx_count, x_length, mode_block)
    table_y, inverse_y, along_x = map(jnp.asarray, (table_y, inverse_y, along_x))
    weights = mode_weights.reshape(-1, width)
    scaled = lambda kernel: lambda *refs: kernel(norm_scale, *refs)
    rows = kx_count * mode_block
    planar = (mode_total, width)
    stacked = (2 * KY, last_width)
    mine = lax.axis_index("sa")
    core, place, field = lax.optimization_barrier(
        (jnp.bitwise_and(mine, 1).reshape(1), jnp.right_shift(mine, 1).reshape(1), field)
    )

    modes, field, table_y, weights, along_x, inverse_y, point_weights = call_first(
        (field, table_y, weights, along_x, inverse_y, point_weights), planar, [stacked, planar]
    )
    coeffs_in, planes, cotangent_rows = call(
        scaled(mix_forward_kernel),
        (exchange(modes), along_x, weights),
        [(rows, width), planar],
        [(rows, width)],
        "mix_forward",
        brought=cotangent_rows,
    )
    modes, field_out, out_grad = call(
        scaled(middle_kernel),
        (exchange(planes), inverse_y, table_y, point_weights, field, cotangent_rows),
        [planar, field.shape, field.shape],
        [stacked, stacked, planar],
        "middle",
        stored=1,
    )
    kept, given, planes = call(
        lambda *refs: mix_backward_kernel(norm_scale, samples, *refs),
        (exchange(modes), along_x, weights, coeffs_in),
        [(rows, width), (rows, width), planar],
        [(rows, width)],
        "mix_backward",
        (core,),
        stored=2,
    )
    arrived = swap_samples(kept, given, place)
    (field_grad,) = call(
        scaled(last_kernel),
        (exchange(planes), inverse_y, point_weights, out_grad),
        [field.shape],
        [stacked, planar],
        "last",
        stored=0,
    )
    arrived, field_grad = lax.optimization_barrier((arrived, field_grad))
    shared = jnp.concatenate(arrived, 0).reshape(samples, 2, kx_count // samples, mode_block, width)
    weight_grad = sample_sum(shared[:, 0], shared[:, 1])
    return (
        field_out.reshape(field_in.shape),
        field_grad.reshape(field_in.shape),
        weight_grad,
    )


def solution(mesh):
    in_specs = (
        P("sa", "gx", None, None),
        P("sa", "gx", None, None),
        P(None, "gx", None, None),
        P(),
    )
    out_specs = (P("sa", "gx", None, None), P("sa", "gx", None, None), P("sa", "gx", None, None))
    return jax.shard_map(
        on_device, mesh=mesh, in_specs=in_specs, out_specs=out_specs, check_vma=False
    )
```

```python
import math

import jax
import jax.numpy as jnp
import numpy as np
from jax import lax
from jax.experimental import pallas as pl
from jax.experimental.pallas import tpu as pltpu
from jax.sharding import PartitionSpec as P

KY = 32
KZ = 16
GELU_COEF = 0.044715
FIRST_BYTES = 16 << 20
SMALL_BYTES = 16 << 20
PIECES = 4
SORT_HINT = 40_000_000_000


def angles(freq_count, grid_count):
    frequency = np.arange(freq_count) - freq_count // 2
    turn_index = np.mod(frequency[:, None] * np.arange(grid_count)[None, :], grid_count)
    return turn_index.astype(np.float32) * np.float32(2.0 * math.pi / grid_count)


def tables_y(y_count):
    theta = angles(KY, y_count)
    return np.concatenate([np.cos(theta), -np.sin(theta)], 0).astype(np.float32)


def forward_table_y(y_count):
    return tables_y(y_count).astype(jnp.bfloat16)


def inverse_table_y(y_count):
    table = tables_y(y_count).T
    high = table.astype(jnp.bfloat16)
    low = (table - high.astype(np.float32)).astype(jnp.bfloat16)
    return np.concatenate([high, high, low], 1)


def table_x(kx_count, x_length, mode_block):
    theta = angles(kx_count, x_length)
    same = np.eye(mode_block, dtype=np.float32)
    cos_wide = np.kron(np.cos(theta), same)
    sin_wide = np.kron(np.sin(theta), same)
    return np.concatenate([cos_wide, sin_wide], 0).astype(jnp.bfloat16)


def dot(left, right):
    return jnp.dot(left, right, preferred_element_type=jnp.float32)


def lanes_of(shape):
    return lax.broadcasted_iota(jnp.int32, shape, 1)


def halves_swapped(pair):
    return pltpu.roll(pair, pair.shape[1] // 2, 1)


def quarter_turn(pair, sign):
    low = lanes_of(pair.shape) < pair.shape[1] // 2
    swapped = halves_swapped(pair)
    return jnp.where(low, -swapped, swapped) if sign > 0 else jnp.where(low, swapped, -swapped)


def fourier(parts, sign):
    count = len(parts)
    if count == 1:
        return parts
    even = fourier(parts[0::2], sign)
    odd = fourier(parts[1::2], sign)
    lower, upper = [], []
    for k in range(count // 2):
        turned = odd[k]
        if 4 * k == count:
            turned = quarter_turn(turned, sign)
        elif k:
            angle = 2.0 * math.pi * k / count
            turned = math.cos(angle) * turned + math.sin(angle) * quarter_turn(turned, sign)
        lower.append(even[k] + turned)
        upper.append(even[k] - turned)
    return lower + upper


class Fetched:
    def __init__(self, source, target, semaphores, first, pieces=1, axis=0):
        size = source.shape[axis] // pieces
        self.copies = []
        for at in range(pieces):
            part = pl.ds(at * size, size)
            index = (part,) if axis == 0 else (slice(None), part)
            self.copies.append(
                pltpu.make_async_copy(source.at[index], target.at[index], semaphores.at[first + at])
            )

    def start(self, at=None):
        for copy in self.copies if at is None else self.copies[at : at + 1]:
            copy.start()

    def wait(self, at=None):
        for copy in self.copies if at is None else self.copies[at : at + 1]:
            copy.wait()


def modes_from(first_pass, wide_modes, modes_out):
    width = modes_out.shape[1]
    low = lanes_of((8, width)) < width // 2
    for block in range(KY // 8):
        parts = []
        for column in range(KZ // 2):
            lanes = pl.ds(column * width, width)
            real = first_pass[pl.ds(block * 8, 8), lanes]
            imag = first_pass[pl.ds(KY + block * 8, 8), lanes]
            parts.append(jnp.where(low, real, halves_swapped(imag)))
            parts.append(jnp.where(low, halves_swapped(real), imag))
        spectrum = fourier(parts, -1)
        for kz in range(KZ):
            wide_modes[pl.ds(block * 8 * KZ + kz, 8, stride=KZ), :] = spectrum[(kz + KZ // 2) % KZ]
        rows = pl.ds(block * 8 * KZ, 8 * KZ)
        modes_out[rows, :] = wide_modes[rows, :].astype(modes_out.dtype)


def stacked_from(planes, wide_modes, stacked, norm_scale):
    width = planes.shape[1]
    low = lanes_of((8, width)) < width // 2
    wide_modes[...] = planes[...].astype(jnp.float32)
    for block in range(KY // 8):
        parts = [
            wide_modes[pl.ds(block * 8 * KZ + (k + KZ // 2) % KZ, 8, stride=KZ), :] for k in range(KZ)
        ]
        grid = fourier(parts, 1)
        for column in range(KZ // 2):
            lanes = pl.ds(column * width, width)
            first = grid[2 * column] * norm_scale
            second = grid[2 * column + 1] * norm_scale
            stacked[pl.ds(block * 8, 8), lanes] = jnp.where(low, first, halves_swapped(second))
            stacked[pl.ds(KY + block * 8, 8), lanes] = jnp.where(low, halves_swapped(first), second)


def three_terms(stacked, lanes):
    value = stacked[:, lanes]
    high = value.astype(jnp.bfloat16)
    low = (value - high.astype(jnp.float32)).astype(jnp.bfloat16)
    return jnp.concatenate([high, low, high], 0)


def paired_of(point_weights):
    channels = point_weights.shape[0]
    wide = jnp.concatenate([point_weights[...].astype(jnp.float32)] * 4, 1)
    tall = jnp.concatenate([wide] * 4, 0)
    row = lax.broadcasted_iota(jnp.int32, tall.shape, 0)
    return jnp.where(row // channels == lanes_of(tall.shape) // channels, tall, 0.0).astype(jnp.bfloat16)


def forward_yz_kernel(*refs):
    count = (len(refs) - 4) // 2
    sources, (modes_out, *targets) = refs[:count], refs[count : 2 * count + 1]
    first_pass, wide_modes, semaphores = refs[2 * count + 1 :]
    fetches = [
        Fetched(source, target, semaphores, at, PIECES if at == 0 else 1, 1)
        if at == 0
        else Fetched(source, target, semaphores, PIECES * (1 + at), PIECES if source.shape[0] >= 256 else 1)
        for at, (source, target) in enumerate(zip(sources, targets))
    ]
    fetches[1].start()
    fetches[0].start()
    for fetch in fetches[2:]:
        fetch.start()
    field, table_y = targets[:2]
    fetches[1].wait()
    width = field.shape[1] // PIECES
    for column in range(PIECES):
        lanes = pl.ds(column * width, width)
        fetches[0].wait(column)
        first_pass[:, lanes] = dot(table_y[...], field[:, lanes])
    modes_from(first_pass, wide_modes, modes_out)
    for fetch in fetches[2:]:
        fetch.wait()


def middle_kernel(
    norm_scale, planes, inverse_y, table_y, point_weights, field, cotangent,
    modes_out, field_out_hbm, out_grad, stacked, first_pass, wide_modes, field_out, semaphores,
):
    store = Fetched(field_out, field_out_hbm, semaphores, 0, PIECES, 1)
    paired = paired_of(point_weights)
    stacked_from(planes, wide_modes, stacked, norm_scale)
    root_const = math.sqrt(2.0 / math.pi)
    width = field.shape[1] // PIECES
    rows_per = 64
    for column in range(PIECES):
        lanes = pl.ds(column * width, width)
        terms = three_terms(stacked, lanes)
        for start in range(0, field.shape[0], rows_per):
            rows = pl.ds(start, rows_per)
            pre_act = dot(inverse_y[rows, :], terms) + dot(field[rows, lanes], paired)
            square = pre_act * pre_act
            tangent = jnp.tanh(pre_act * (root_const + root_const * GELU_COEF * square))
            half = 0.5 + 0.5 * tangent
            activated = pre_act * half
            slope = half + activated * (1.0 - tangent) * (root_const + 3.0 * root_const * GELU_COEF * square)
            field_out[rows, lanes] = activated.astype(field_out.dtype)
            out_grad[rows, lanes] = (cotangent[rows, lanes].astype(jnp.float32) * slope).astype(out_grad.dtype)
        store.start(column)
        first_pass[:, lanes] = dot(table_y[...], out_grad[:, lanes])
    modes_from(first_pass, wide_modes, modes_out)
    store.wait()


def last_kernel(
    norm_scale, planes, inverse_y, point_weights, out_grad,
    field_grad_hbm, stacked, wide_modes, field_grad, semaphores,
):
    store = Fetched(field_grad, field_grad_hbm, semaphores, 0, PIECES, 1)
    paired = paired_of(point_weights)
    stacked_from(planes, wide_modes, stacked, norm_scale)
    width = paired.shape[0]
    rows_per = 128
    for column in range(PIECES):
        lanes = pl.ds(column * width, width)
        terms = three_terms(stacked, lanes)
        for start in range(0, out_grad.shape[0], rows_per):
            rows = pl.ds(start, rows_per)
            mixed = lax.dot_general(
                out_grad[rows, lanes], paired, (((1,), (1,)), ((), ())), preferred_element_type=jnp.float32
            )
            field_grad[rows, lanes] = (dot(inverse_y[rows, :], terms) + mixed).astype(field_grad.dtype)
        store.start(column)
    store.wait()


def coeffs_of(along_x, mode_data, norm_scale):
    both = dot(along_x[...], mode_data[...])
    count = both.shape[0] // 2
    return ((both[:count] + quarter_turn(both[count:], -1)) * norm_scale).astype(jnp.bfloat16)


def store_planes(along_x, mixed, planes_out, store=None):
    mixed = mixed[...]
    turned = quarter_turn(mixed.astype(jnp.bfloat16).astype(jnp.float32), 1).astype(jnp.bfloat16)
    terms = jnp.concatenate([mixed.astype(jnp.bfloat16), turned], 0)
    size = planes_out.shape[0] // PIECES
    for piece in range(PIECES):
        rows = pl.ds(piece * size, size)
        planes_out[rows, :] = lax.dot_general(
            along_x[:, rows], terms, (((0,), (0,)), ((), ())), preferred_element_type=jnp.float32
        ).astype(jnp.bfloat16)
        if store is not None:
            store.start(piece)
    if store is not None:
        store.wait()


def own_block(shape, channels):
    row = lax.broadcasted_iota(jnp.int32, shape, 0)
    return lanes_of(shape) // channels == row % 8


def mixed_forward(coeffs, weights, mixed):
    count, width = coeffs.shape
    channels = width // 2
    mine = own_block((8, 8 * channels), channels)
    low = lanes_of((8, width)) < channels
    for start in range(0, count, 8):
        pair = coeffs[start : start + 8].astype(jnp.float32)
        swapped = halves_swapped(pair)
        real = jnp.where(low, pair, swapped)
        imag = jnp.where(low, swapped, pair)
        spread = jnp.concatenate(
            [jnp.where(mine, jnp.concatenate([part] * 4, 1), 0.0) for part in (real, imag)], 0
        ).astype(jnp.bfloat16)
        both = dot(spread, weights[pl.ds(start * channels, 8 * channels), :])
        mixed[pl.ds(start, 8), :] = both[:8] + quarter_turn(both[8:], 1)


def mixed_backward(coeffs, weights, mixed):
    count, width = coeffs.shape
    channels = width // 2
    mine = own_block((8, 8 * channels), channels)
    low = lanes_of((8, width)) < channels
    for start in range(0, count, 8):
        pair = coeffs[start : start + 8].astype(jnp.float32)
        sides = jnp.concatenate([pair, quarter_turn(pair, -1)], 0).astype(jnp.bfloat16)
        every = lax.dot_general(
            sides,
            weights[pl.ds(start * channels, 8 * channels), :],
            (((1,), (1,)), ((), ())),
            preferred_element_type=jnp.float32,
        )
        folded = []
        for half in (every[:8], every[8:]):
            own = jnp.where(mine, half, 0.0)
            total = sum(own[:, at * width : (at + 1) * width] for at in range(4))
            folded.append(total + halves_swapped(total))
        mixed[pl.ds(start, 8), :] = jnp.where(low, folded[0], folded[1])


def mix_forward_kernel(
    norm_scale, mode_data, along_x, weights, later_hbm, coeffs_out, planes_out, later, mixed, semaphores
):
    fetch = Fetched(later_hbm, later, semaphores, 0)
    fetch.start()
    coeffs = coeffs_of(along_x, mode_data, norm_scale)
    coeffs_out[...] = coeffs
    mixed_forward(coeffs, weights, mixed)
    store_planes(along_x, mixed, planes_out)
    fetch.wait()


def mix_backward_kernel(
    norm_scale, samples, core, mode_data, along_x, weights, coeffs_in,
    kept, given, planes_hbm, mixed, planes_out, semaphores,
):
    store = Fetched(planes_out, planes_hbm, semaphores, 0, PIECES)
    coeffs = coeffs_of(along_x, mode_data, norm_scale)
    first_core = core[0] == 0
    size = coeffs.shape[0] // samples
    for side, values in enumerate((coeffs_in[...], coeffs)):
        for place in range(samples // 2):
            even = values[2 * place * size : (2 * place + 1) * size].astype(jnp.float32)
            odd = values[(2 * place + 1) * size : (2 * place + 2) * size].astype(jnp.float32)
            rows = pl.ds((side * (samples // 2) + place) * size, size)
            kept[rows, :] = jnp.where(first_core, even, odd).astype(jnp.bfloat16)
            given[rows, :] = jnp.where(first_core, odd, even).astype(jnp.bfloat16)
    mixed_backward(coeffs, weights, mixed)
    store_planes(along_x, mixed, planes_out, store)


def call_first(operands, modes_shape, scratch):
    outs = [jax.ShapeDtypeStruct(modes_shape, jnp.bfloat16)] + [
        jax.ShapeDtypeStruct(array.shape, array.dtype) for array in operands
    ]
    return pl.pallas_call(
        forward_yz_kernel,
        name="forward_yz",
        out_shape=outs,
        in_specs=[pl.BlockSpec(memory_space=pltpu.HBM)] * len(operands),
        out_specs=[pl.BlockSpec(memory_space=pltpu.VMEM)] * len(outs),
        scratch_shapes=[pltpu.VMEM(shape, jnp.float32) for shape in scratch]
        + [pltpu.SemaphoreType.DMA((PIECES * (1 + len(operands)),))],
        compiler_params=pltpu.CompilerParams(vmem_limit_bytes=FIRST_BYTES),
    )(*(pltpu.with_memory_space_constraint(array, pltpu.HBM) for array in operands))


def call(kernel, operands, outs, scratch, name, scalars=(), estimate=None, stored=None, brought=None):
    whole = pl.BlockSpec(memory_space=pltpu.VMEM)
    out_specs = [whole] * len(outs)
    scratch_shapes = [pltpu.VMEM(shape, jnp.float32) for shape in scratch]
    if stored is not None:
        out_specs[stored] = pl.BlockSpec(memory_space=pl.ANY)
        scratch_shapes += [pltpu.VMEM(outs[stored], jnp.bfloat16), pltpu.SemaphoreType.DMA((PIECES,))]
    in_specs = [pl.BlockSpec(memory_space=pltpu.SMEM)] * len(scalars) + [whole] * len(operands)
    if brought is not None:
        operands = (*operands, pltpu.with_memory_space_constraint(brought, pltpu.HBM))
        in_specs.append(pl.BlockSpec(memory_space=pltpu.HBM))
        outs = [*outs, brought.shape]
        out_specs.append(whole)
        scratch_shapes.append(pltpu.SemaphoreType.DMA((1,)))
    return pl.pallas_call(
        kernel,
        name=name,
        cost_estimate=estimate,
        out_shape=[jax.ShapeDtypeStruct(shape, jnp.bfloat16) for shape in outs],
        in_specs=in_specs,
        out_specs=out_specs,
        scratch_shapes=scratch_shapes,
        compiler_params=pltpu.CompilerParams(vmem_limit_bytes=SMALL_BYTES),
    )(*scalars, *operands)


def exchange(rows):
    count = lax.axis_size("gx")
    slots = rows.reshape(count, rows.shape[0] // count, rows.shape[1])
    return lax.all_to_all(slots, "gx", split_axis=0, concat_axis=0, tiled=True).reshape(rows.shape)


def sort_kernel(place, kept, taken, *blocks):
    size = kept.shape[0] // (2 * len(blocks))
    for step, block in enumerate(blocks):
        wanted = jnp.bitwise_xor(place[0], step)
        for core, source in enumerate((kept, taken)):
            for side in range(2):
                start = pl.multiple_of((side * len(blocks) + wanted) * size, size)
                block[pl.ds((2 * core + side) * size, size), :] = source[pl.ds(start, size), :]


def swap_samples(kept, given, place):
    count = lax.axis_size("sa")
    taken = lax.ppermute(given, "sa", [(i, i ^ 1) for i in range(count)])
    rows, width = kept.shape
    blocks = call(
        sort_kernel,
        (kept, taken),
        [(4 * rows // count, width)] * (count // 2),
        [],
        "sort",
        (place,),
        pl.CostEstimate(flops=SORT_HINT, bytes_accessed=4 * rows * width, transcendentals=0),
    )
    return [blocks[0]] + [
        lax.ppermute(blocks[step], "sa", [(i, i ^ 2 * step) for i in range(count)])
        for step in range(1, count // 2)
    ]


def sample_sum(left_side, right_side):
    samples, kx_count, mode_block, width = left_side.shape
    channels = width // 2
    left = left_side.reshape(samples, kx_count, mode_block, 2, channels)
    swapped = jnp.concatenate([right_side[..., channels:], -right_side[..., :channels]], -1)
    right = jnp.stack([right_side, swapped], 3)
    return jnp.einsum("skmtc,skmtp->kmcp", left, right, preferred_element_type=jnp.float32)


def on_device(field_in, cotangent, mode_weights, point_weights):
    field = field_in.reshape(field_in.shape[-2:])
    cotangent_rows = cotangent.reshape(field.shape)
    y_count, last_width = field.shape
    channels = point_weights.shape[0]
    kx_count, mode_block = mode_weights.shape[:2]
    x_length = lax.axis_size("gx")
    samples = lax.axis_size("sa")
    z_count = last_width // channels
    norm_scale = 1.0 / math.sqrt(x_length * y_count * z_count)
    width = 2 * channels
    mode_total = KY * KZ
    table_y = forward_table_y(y_count)
    inverse_y = inverse_table_y(y_count)
    along_x = table_x(kx_count, x_length, mode_block)
    table_y, inverse_y, along_x = map(jnp.asarray, (table_y, inverse_y, along_x))
    weights = mode_weights.reshape(-1, width)
    scaled = lambda kernel: lambda *refs: kernel(norm_scale, *refs)
    rows = kx_count * mode_block
    planar = (mode_total, width)
    stacked = (2 * KY, last_width)
    mine = lax.axis_index("sa")
    core, place, field = lax.optimization_barrier(
        (jnp.bitwise_and(mine, 1).reshape(1), jnp.right_shift(mine, 1).reshape(1), field)
    )

    modes, field, table_y, weights, along_x, inverse_y, point_weights = call_first(
        (field, table_y, weights, along_x, inverse_y, point_weights), planar, [stacked, planar]
    )
    coeffs_in, planes, cotangent_rows = call(
        scaled(mix_forward_kernel),
        (exchange(modes), along_x, weights),
        [(rows, width), planar],
        [(rows, width)],
        "mix_forward",
        brought=cotangent_rows,
    )
    modes, field_out, out_grad = call(
        scaled(middle_kernel),
        (exchange(planes), inverse_y, table_y, point_weights, field, cotangent_rows),
        [planar, field.shape, field.shape],
        [stacked, stacked, planar],
        "middle",
        stored=1,
    )
    kept, given, planes = call(
        lambda *refs: mix_backward_kernel(norm_scale, samples, *refs),
        (exchange(modes), along_x, weights, coeffs_in),
        [(rows, width), (rows, width), planar],
        [(rows, width)],
        "mix_backward",
        (core,),
        stored=2,
    )
    arrived = swap_samples(kept, given, place)
    (field_grad,) = call(
        scaled(last_kernel),
        (exchange(planes), inverse_y, point_weights, out_grad),
        [field.shape],
        [stacked, planar],
        "last",
        stored=0,
    )
    arrived, field_grad = lax.optimization_barrier((arrived, field_grad))
    shared = jnp.concatenate(arrived, 0).reshape(samples, 2, kx_count // samples, mode_block, width)
    weight_grad = sample_sum(shared[:, 0], shared[:, 1])
    return (
        field_out.reshape(field_in.shape),
        field_grad.reshape(field_in.shape),
        weight_grad,
    )


def solution(mesh):
    in_specs = (
        P("sa", "gx", None, None),
        P("sa", "gx", None, None),
        P(None, "gx", None, None),
        P(),
    )
    out_specs = (P("sa", "gx", None, None), P("sa", "gx", None, None), P("sa", "gx", None, None))
    return jax.shard_map(
        on_device, mesh=mesh, in_specs=in_specs, out_specs=out_specs, check_vma=False
    )
```
